128 devices in a mesh: site: 4 (over y), term: 32 (over z, x, core).
Axes of the slice: x: 4, y: 4, z: 4, core: 2. Of those that a mesh axis runs over, the one named last changes fastest.
Arguments:
- left_env: float32 [32, 12, 256, 256], P('term'), may hold values from -6 to 6
- right_env: float32 [4, 32, 12, 256, 256], P('site', 'term'), may hold values from -6 to 6
- mps: float32 [4, 2, 12, 256, 256], P('site'), may hold values from -0.375 to 0.375
- psi: float32 [4, 2, 12, 256, 256], P('site'), may hold values from -0.00390625 to 0.00390625
- coef: float32 [4, 32, 4], P('site', 'term'), may hold values from 0.5 to 1.5
- sector_sizes: int32 [12], replicated, may hold values from 128 to 256, as said below
- pattern: int32 [32, 12], P('term'), may hold values 0 or 1
Outputs:
- applied: float32 [4, 2, 3072, 256], P('site', None, 'term')
The draws below stay inside these ranges and needn't reach their ends.
Inputs may be any that keep to these rules, and one draw needn't show every extreme that they name: `sector_sizes`: every size lies in 128 .. 256, the sizes add up to exactly 2560, and at least one sector has exactly 256.
All inputs are finite; a program needn't handle non-finite values. No bound on the sum of `pattern` on one device may be relied on, other than what follows from the above.
Results may differ from the reference program's by a relative error of at most 0.00018.
Values sent between devices are 32-bit elements; how exact they have to be, the bound alone decides.
No kernel may reach another device: no remote copies, remote signals or barrier semaphores. Data moves between devices by JAX's collectives and lax.ppermute only.
A program may use at most 128 MiB of HBM per device.

```python
import jax
import jax.numpy as jnp
from jax import lax

NSEC = 12
P_SIZE = 256
BOND = 2560
TERMS = 32
N_SITE = 4


def draw_sector_sizes(key, part):
    first_key, second_key = jax.random.split(jax.random.fold_in(key, 17))
    lowest = P_SIZE // 2
    spare_rows = BOND - NSEC * lowest - lowest
    full_slot = jax.random.randint(first_key, (), 0, NSEC)
    unit_slots = jax.random.permutation(second_key, (NSEC - 1) * lowest)[:spare_rows] // lowest
    counts_other = jnp.sum((unit_slots[None, :] == jnp.arange(NSEC - 1)[:, None]).astype(jnp.int32), axis=1)
    others = lowest + counts_other
    slot_index = jnp.arange(NSEC)
    source = jnp.clip(slot_index - (slot_index > full_slot).astype(jnp.int32), 0, NSEC - 2)
    return jnp.where(slot_index == full_slot, P_SIZE, others[source]).astype(jnp.int32)


def plant(entries, own_key, low, top_value):
    dims = entries.shape
    place = [jax.random.randint(jax.random.fold_in(own_key, axis), (), 0, dims[axis]) for axis in range(len(dims))]
    entries = entries.at[tuple(place)].set(low)
    longest = dims.index(max(dims))
    place[longest] = (place[longest] + 1) % dims[longest]
    return entries.at[tuple(place)].set(top_value)


def level_of(stream_key, shape, cuts, low, top_value):
    gain = 1.0
    for position, blocks in cuts:
        heights = jax.random.uniform(jax.random.fold_in(jax.random.fold_in(stream_key, 6), position), (blocks,), jnp.float32, low / len(cuts), top_value / len(cuts))
        gain = gain * jnp.repeat(jnp.exp(heights), shape[position] // blocks).reshape((-1,) + (1,) * (len(shape) - 1 - position))
    return gain


def normal_values(own_key, dims, width, most, cuts=(), held_as=jnp.bfloat16):
    factor_of = level_of(own_key, dims, cuts, -0.22, 0.18) if cuts else 1.0
    drawn = jax.random.normal(own_key, dims, jnp.float32) * width * factor_of
    return jnp.minimum(jnp.maximum(drawn, -most), most).astype(held_as)


def setup_inputs(seed: int = 0) -> dict:
    splits = jax.random.split(jax.random.key(seed), 8)
    return {
        "left_env": normal_values(splits[0], (TERMS, NSEC, P_SIZE, P_SIZE), 1.0, 6.0, ((0, 32),), jnp.float32),
        "right_env": normal_values(splits[1], (N_SITE, TERMS, NSEC, P_SIZE, P_SIZE), 1.0, 6.0, ((0, 4), (1, 32)), jnp.float32),
        "mps": normal_values(splits[2], (N_SITE, 2, NSEC, P_SIZE, P_SIZE), P_SIZE ** -0.5, 0.375, ((0, 4),), jnp.float32),
        "psi": normal_values(splits[3], (N_SITE, 2, NSEC, P_SIZE, P_SIZE), (P_SIZE * P_SIZE * TERMS) ** -0.5, 0.00390625, ((0, 4),), jnp.float32),
        "coef": jnp.clip(0.5 + 1.0 * jax.random.uniform(splits[4], (N_SITE, TERMS, 4), jnp.float32) ** level_of(splits[4], (N_SITE, TERMS, 4), ((0, 4), (1, 32)), -0.2, 0.2), 0.5, 1.5),
        "sector_sizes": draw_sector_sizes(jax.random.fold_in(splits[7], 71), 0),
        "pattern": plant((jax.random.randint(splits[6], (TERMS, NSEC), 0, 4) < 3).astype(jnp.int32), jax.random.fold_in(splits[6], 1), 0, 1),
    }


highest = lax.Precision.HIGHEST


def live_masks(sector_sizes):
    live_rows = (jnp.arange(P_SIZE)[None, :] < sector_sizes[:, None]).astype(jnp.float32)
    following = jnp.concatenate([live_rows[1:], jnp.zeros((1, P_SIZE), jnp.float32)], axis=0)
    sector_frame = live_rows[:, :, None] * live_rows[:, None, :]
    step_frame = live_rows[:, :, None] * following[:, None, :]
    return sector_frame, step_frame


def sandwich(blocks, tensors):
    product = jnp.einsum("nij,njk->nik", blocks, tensors, precision=highest)
    return jnp.einsum("nim,nik->nmk", tensors, product, precision=highest)


def advance(environ, weights, same_state, next_state):
    shifted = jnp.concatenate([jnp.zeros((1, P_SIZE, P_SIZE), jnp.float32), environ[:-1]], axis=0)
    rolled = jnp.roll(next_state, 1, axis=0)
    return weights[0] * sandwich(environ, same_state) + weights[1] * sandwich(shifted, rolled)


def reference(left_env, right_env, mps, psi, coef, sector_sizes, pattern):
    sector_frame, step_frame = live_masks(sector_sizes)
    presence = pattern.astype(jnp.float32)[:, :, None, None]
    environ = left_env * sector_frame[None] * presence
    results = []
    for section_index in range(N_SITE):
        same_state = mps[section_index, 0] * sector_frame
        next_state = mps[section_index, 1] * step_frame

        def update_term(operands):
            return advance(operands[0], operands[1], same_state, next_state)

        environ = lax.map(update_term, (environ, coef[section_index]))
        rights = right_env[section_index] * sector_frame[None] * presence
        first_psi = psi[section_index, 0] * sector_frame
        second_psi = psi[section_index, 1] * step_frame

        def accumulate(totals, pieces):
            left_blocks, right_blocks, weights = pieces
            upper_blocks = jnp.concatenate([right_blocks[1:], jnp.zeros((1, P_SIZE, P_SIZE), jnp.float32)], axis=0)
            first_term = jnp.einsum("qij,qjk->qik", left_blocks, first_psi, precision=highest)
            first_term = jnp.einsum("qik,qlk->qil", first_term, right_blocks, precision=highest)
            second = jnp.einsum("qij,qjk->qik", left_blocks, second_psi, precision=highest)
            second = jnp.einsum("qik,qlk->qil", second, upper_blocks, precision=highest)
            return (totals[0] + weights[2] * first_term, totals[1] + weights[3] * second), None

        empty_sum = jnp.zeros((NSEC, P_SIZE, P_SIZE), jnp.float32)
        sums, ignored = lax.scan(accumulate, (empty_sum, empty_sum), (environ, rights, coef[section_index]))
        results.append(jnp.stack([sums[0].reshape(NSEC * P_SIZE, P_SIZE), sums[1].reshape(NSEC * P_SIZE, P_SIZE)]))
    return jnp.stack(results)
```

```python
import jax
import jax.numpy as jnp
from jax import lax
from jax.experimental import pallas as pl
from jax.experimental.pallas import tpu as pltpu
from jax.sharding import Mesh, PartitionSpec as P

f32, bf16 = jnp.float32, jnp.bfloat16
W = 256
NQ = 12
ROWS = 32
HEAVY = pltpu.CompilerParams(dimension_semantics=("arbitrary",), vmem_limit_bytes=48 * 2**20)


def halves(x):
    high = x.astype(bf16)
    return high, (x - high.astype(f32)).astype(bf16)


def product(a, b, dims):
    (ah, al), (bh, bl) = a, b

    def dot(u, v):
        return lax.dot_general(u, v, (dims, ((), ())), preferred_element_type=f32)

    return dot(ah, bh) + (dot(ah, bl) + dot(al, bh))


def framed(x, rows, columns):
    i = lax.broadcasted_iota(jnp.int32, x.shape, 0)
    j = lax.broadcasted_iota(jnp.int32, x.shape, 1)
    return jnp.where((i < rows) & (j < columns), x, 0.0)


def update_kernel(stage, ints, floats, same, before, s_ref, u_ref, out):
    r = pl.program_id(0)
    site = ints[0]

    @pl.when(site < stage)
    def _():
        out[...] = same[...]

    @pl.when(site >= stage)
    def _():
        below = jnp.maximum(r - 1, 0)
        c0, c1 = floats[4 * stage], floats[4 * stage + 1]
        if stage == 0:
            c0 = c0 * ints[14 + r].astype(f32)
            c1 = c1 * ints[14 + below].astype(f32)
        c1 = jnp.where(r > 0, c1, 0.0)
        size, under = ints[1 + r], ints[1 + below]
        s = framed(s_ref[0, 0], size, size)
        u = framed(u_ref[0, 0], under, size)
        first = c0 * product(halves(same[0]), halves(s), ((1,), (0,)))
        second = c1 * product(halves(before[0]), halves(u), ((1,), (0,)))
        out[0] = product(halves(s.T), halves(first), ((1,), (0,))) + product(
            halves(u.T), halves(second), ((1,), (0,)))


def update(stage, ints, floats, environ, tensors):
    block = (1, W, W)
    pair = (1, 1, W, W)

    def kernel(*refs):
        update_kernel(stage, *refs)

    def below(r, *_):
        return (jnp.maximum(r - 1, 0), 0, 0)

    spec = pltpu.PrefetchScalarGridSpec(
        num_scalar_prefetch=2, grid=(NQ,),
        in_specs=[
            pl.BlockSpec(block, lambda r, *_: (r, 0, 0)),
            pl.BlockSpec(block, below),
            pl.BlockSpec(pair, lambda r, *_: (0, r, 0, 0)),
            pl.BlockSpec(pair, lambda r, *_: (1, jnp.maximum(r - 1, 0), 0, 0)),
        ],
        out_specs=pl.BlockSpec(block, lambda r, *_: (r, 0, 0)),
    )
    return pl.pallas_call(
        kernel, grid_spec=spec, out_shape=jax.ShapeDtypeStruct((NQ, W, W), f32),
        compiler_params=HEAVY, name=f"update{stage}",
    )(ints, floats, environ, environ, tensors, tensors)


def apply_kernel(ints, floats, env, x0, x1, g0, g1, keep, send):
    q = pl.program_id(0)
    above = jnp.minimum(q + 1, NQ - 1)
    core = ints[26]
    present = ints[14 + q].astype(f32)
    present_above = jnp.where(q < NQ - 1, ints[14 + above], 0).astype(f32)
    site = ints[0]
    c2 = floats[4 * site + 2] * present
    c3 = floats[4 * site + 3] * present_above
    e = halves(env[0])
    size, over = ints[1 + q], ints[1 + above]
    results = []
    for x, g, c, n in ((x0, g0, c2, size), (x1, g1, c3, over)):
        part = c * product(e, halves(x[0, 0]), ((1,), (0,)))
        results.append(product(halves(part), halves(framed(g[0], n, n)), ((1,), (1,))))
    for i in range(W // ROWS):
        piece = (W // ROWS) * q + i
        owner, third = piece // 3, piece % 3
        oz, ox, oc = owner // 8, (owner // 2) % 4, owner % 2
        rows = slice(ROWS * i, ROWS * (i + 1))

        def store(target):
            target[0, ox, oz, third] = results[0][rows]
            target[1, oz, ox, third] = results[1][rows]

        @pl.when(oc == core)
        def _():
            store(keep)

        @pl.when(oc != core)
        def _():
            store(send)


def apply(ints, floats, environ, psi, rights):
    pair = (1, 1, W, W)
    shape = (2, 4, 4, 3, ROWS, W)

    def above(q, *_):
        return (jnp.minimum(q + 1, NQ - 1), 0, 0)

    whole = pl.BlockSpec(shape, lambda q, *_: (0,) * 6)
    spec = pltpu.PrefetchScalarGridSpec(
        num_scalar_prefetch=2, grid=(NQ,),
        in_specs=[
            pl.BlockSpec((1, W, W), lambda q, *_: (q, 0, 0)),
            pl.BlockSpec(pair, lambda q, *_: (0, q, 0, 0)),
            pl.BlockSpec(pair, lambda q, *_: (1, q, 0, 0)),
            pl.BlockSpec((1, W, W), lambda q, *_: (q, 0, 0)),
            pl.BlockSpec((1, W, W), above),
        ],
        out_specs=[whole, whole],
    )
    return pl.pallas_call(
        apply_kernel, grid_spec=spec, out_shape=[jax.ShapeDtypeStruct(shape, f32)] * 2,
        compiler_params=HEAVY, name="apply",
    )(ints, floats, environ, psi, psi, rights, rights)


def exchanged(x, axis):
    return jnp.sum(lax.all_to_all(x, axis, 0, 0, tiled=True), axis=0)


def reduced(keep, send):
    both = keep + lax.ppermute(send, "core", [(0, 1), (1, 0)])
    both = both.reshape(2, 4, 4, 96, W)
    first = exchanged(both[0], "x")
    second = exchanged(both[1], "z")
    return jnp.stack([exchanged(first, "z"), exchanged(second, "x")])[None]


def shards(left_env, right_env, mps, psi, coef, sector_sizes, pattern):
    site = lax.axis_index("site").astype(jnp.int32)
    core = lax.axis_index("core").astype(jnp.int32)
    ints = jnp.concatenate([site[None], sector_sizes, jnp.zeros((1,), jnp.int32), pattern[0], core[None]])
    floats = lax.all_gather(coef[0, 0], "site", axis=0, tiled=True)
    tensors = lax.all_gather(mps, "site", axis=0, tiled=True)
    environ = left_env[0]
    for stage in range(4):
        environ = update(stage, ints, floats, environ, tensors[stage])
    keep, send = apply(ints, floats, environ, psi[0], right_env[0, 0])
    return reduced(keep, send)


def solution(mesh):
    fine = Mesh(mesh.devices.reshape(4, 4, 4, 2), ("site", "z", "x", "core"))
    term = ("z", "x", "core")
    return jax.shard_map(
        shards,
        mesh=fine,
        in_specs=(
            P(term, None, None, None),
            P("site", term, None, None, None),
            P("site", None, None, None, None),
            P("site", None, None, None, None),
            P("site", term, None),
            P(),
            P(term, None),
        ),
        out_specs=P("site", None, term, None),
        check_vma=False,
    )
```

```python
import jax
import jax.numpy as jnp
from jax import lax
from jax.experimental import pallas as pl
from jax.experimental.pallas import tpu as pltpu
from jax.sharding import Mesh, PartitionSpec as P

f32, bf16 = jnp.float32, jnp.bfloat16
W = 256
NQ = 12
ROWS = 32
SITES = 4
LAG = 2


def halves(x):
    high = x.astype(bf16)
    return high, (x - high.astype(f32)).astype(bf16)


def product(a, b, dims):
    (ah, al), (bh, bl) = a, b

    def dot(u, v):
        return lax.dot_general(u, v, (dims, ((), ())), preferred_element_type=f32)

    return dot(ah, bh) + (dot(ah, bl) + dot(al, bh))


def framed(x, rows, columns):
    i = lax.broadcasted_iota(jnp.int32, x.shape, 0)
    j = lax.broadcasted_iota(jnp.int32, x.shape, 1)
    return jnp.where((i < rows) & (j < columns), x, 0.0)


def sector_kernel(step, ints, floats, left, arrived, previous, mps, psi, rights, *rest):
    environ, keep, send, blocks, results, sems, stores = rest[-7:]
    site, my_z, my_x, core = ints[0], ints[1], ints[2], ints[3]
    q = step - LAG * site
    below = jnp.maximum(q - 1, 0)
    above = jnp.minimum(q + 1, NQ - 1)

    def load(source, slot):
        return pltpu.make_async_copy(source, blocks.at[slot], sems.at[slot])

    @pl.when((q >= 0) & (q < NQ))
    def _():
        @pl.when(site == 0)
        def _():
            load(left.at[q], 0).start()
            load(left.at[below], 1).start()

        sources = (mps.at[0, q], mps.at[1, below], psi.at[0, q], psi.at[1, q], rights.at[q], rights.at[above])
        for i, source in enumerate(sources):
            load(source, 2 + i).start()
        size, under, over = ints[4 + q], ints[4 + below], ints[4 + above]
        present, present_above = ints[16 + q].astype(f32), ints[16 + above].astype(f32)
        present_above = jnp.where(q < NQ - 1, present_above, 0.0)
        c0 = jnp.where(site == 0, present, 1.0) * floats[0]
        c1 = jnp.where(site == 0, ints[16 + below].astype(f32), 1.0) * floats[1]
        @pl.when(site == 0)
        def _():
            load(left.at[q], 0).wait()
            load(left.at[below], 1).wait()

        load(left.at[0], 2).wait()
        load(left.at[0], 3).wait()
        now = jnp.where(site == 0, blocks[0], arrived[...])
        before = jnp.where(site == 0, blocks[1], previous[...])
        s = framed(blocks[2], size, size)
        u = framed(blocks[3], under, size)
        before = jnp.where(q > 0, before, 0.0)
        first = c0 * product(halves(now), halves(s), ((1,), (0,)))
        second = c1 * product(halves(before), halves(u), ((1,), (0,)))
        moved = product(halves(s.T), halves(first), ((1,), (0,))) + product(
            halves(u.T), halves(second), ((1,), (0,)))
        environ[...] = moved
        e = halves(moved)
        for i in range(4, 8):
            load(left.at[0], i).wait()
        for state, c, n in ((0, floats[2] * present, size), (1, floats[3] * present_above, over)):
            part = c * product(e, halves(blocks[4 + state]), ((1,), (0,)))
            results[state] = product(halves(part), halves(framed(blocks[6 + state], n, n)), ((1,), (1,)))

        def move(state, i, target, near, far, third):
            return pltpu.make_async_copy(
                results.at[state, pl.ds(ROWS * i, ROWS)], target.at[state, near, far, third], stores)

        for i in range(W // ROWS):
            piece = (W // ROWS) * q + i
            owner, third = piece // 3, piece % 3
            z = (owner // 8 - my_z + 4) % 4
            x = ((owner // 2) % 4 - my_x + 4) % 4
            mine = owner % 2 == core

            @pl.when(mine)
            def _():
                move(0, i, keep, x, z, third).start()
                move(1, i, keep, z, x, third).start()

            @pl.when(jnp.logical_not(mine))
            def _():
                move(0, i, send, x, z, third).start()
                move(1, i, send, z, x, third).start()

        pltpu.make_async_copy(results, blocks.at[pl.ds(0, 2)], stores).wait()


def sector_step(step, ints, floats, left, arrived, previous, mps, psi, rights, held):
    scalar = pl.BlockSpec(memory_space=pltpu.SMEM)
    anywhere = pl.BlockSpec(memory_space=pl.ANY)
    local = pl.BlockSpec(memory_space=pltpu.VMEM)
    shape = jax.ShapeDtypeStruct((2, 4, 4, 3, ROWS, W), f32)

    def kernel(*refs):
        sector_kernel(step, *refs)

    return pl.pallas_call(
        kernel,
        in_specs=[scalar] * 2 + [anywhere] + [local] * 2 + [anywhere] * (3 + len(held)),
        out_specs=[local, anywhere, anywhere],
        out_shape=[jax.ShapeDtypeStruct((W, W), f32), shape, shape],
        scratch_shapes=[
            pltpu.VMEM((8, W, W), f32),
            pltpu.VMEM((2, W, W), f32),
            pltpu.SemaphoreType.DMA((8,)),
            pltpu.SemaphoreType.DMA,
        ],
        input_output_aliases={8: 1, 9: 2} if held else {},
        name=f"sector{step}",
    )(ints, floats, left, arrived, previous, mps, psi, rights, *held)


def turned(x, axis, by):
    return lax.ppermute(x, axis, [(i, (i + by) % 4) for i in range(4)])


def round_far(blocks, axis):
    half = blocks.shape[1] // 2
    up = turned(blocks[2, :half], axis, 1)
    down = turned(blocks[2, half:], axis, -1)
    return blocks[0], jnp.concatenate([blocks[1, :half] + up, blocks[1, half:]]), jnp.concatenate(
        [blocks[3, :half], blocks[3, half:] + down])


def round_near(parts, axis):
    own, ahead, behind = parts
    return own + turned(ahead, axis, 1) + turned(behind, axis, -1)


def reduced(keep, send):
    both = keep + lax.ppermute(send, "core", [(0, 1), (1, 0)])
    both = both.reshape(2, 4, 4, 96, W)
    first, second = round_far(both[0], "x"), round_far(both[1], "z")
    first, second = round_near(first, "x"), round_near(second, "z")
    first, second = round_far(first, "z"), round_far(second, "x")
    return jnp.stack([round_near(first, "z"), round_near(second, "x")])[None]


def shards(left_env, right_env, mps, psi, coef, sector_sizes, pattern):
    place = jnp.stack([lax.axis_index(a) for a in ("site", "z", "x", "core")]).astype(jnp.int32)
    ints = jnp.concatenate([place, sector_sizes, pattern[0]])
    floats = coef[0, 0]
    last = NQ + LAG * (SITES - 1)
    nothing = jnp.zeros((W, W), f32)
    arrivals = {}
    held = ()
    for step in range(last):
        environ, *held = sector_step(
            step, ints, floats, left_env[0], arrivals.get(step, nothing), arrivals.get(step - 1, nothing),
            mps[0], psi[0], right_env[0, 0], tuple(held))
        if step + LAG < last:
            arrivals[step + LAG] = lax.ppermute(environ, "site", [(0, 1), (1, 2), (2, 3)])
    return reduced(*held)


def solution(mesh):
    fine = Mesh(mesh.devices.reshape(4, 4, 4, 2), ("site", "z", "x", "core"))
    term = ("z", "x", "core")
    return jax.shard_map(
        shards,
        mesh=fine,
        in_specs=(
            P(term, None, None, None),
            P("site", term, None, None, None),
            P("site", None, None, None, None),
            P("site", None, None, None, None),
            P("site", term, None),
            P(),
            P(term, None),
        ),
        out_specs=P("site", None, term, None),
        check_vma=False,
    )
```

```python
import jax
import jax.numpy as jnp
from jax import lax
from jax.experimental import pallas as pl
from jax.experimental.pallas import tpu as pltpu
from jax.sharding import Mesh, PartitionSpec as P

f32, bf16 = jnp.float32, jnp.bfloat16
W = 256
NQ = 12
ROWS = 32
SITES = 4
LAG = 2


def halves(x):
    high = x.astype(bf16)
    return high, (x - high.astype(f32)).astype(bf16)


def product(a, b, dims):
    (ah, al), (bh, bl) = a, b

    def dot(u, v):
        return lax.dot_general(u, v, (dims, ((), ())), preferred_element_type=f32)

    return dot(ah, bh) + (dot(ah, bl) + dot(al, bh))


def framed(x, rows, columns):
    i = lax.broadcasted_iota(jnp.int32, x.shape, 0)
    j = lax.broadcasted_iota(jnp.int32, x.shape, 1)
    return jnp.where((i < rows) & (j < columns), x, 0.0)


def fetch(q, left, mps, psi, rights, stage, sems, wait):
    below, above = jnp.maximum(q - 1, 0), jnp.minimum(q + 1, NQ - 1)
    sources = (left.at[q], mps.at[0, q], mps.at[1, below], psi.at[0, q], psi.at[1, q], rights.at[q], rights.at[above], left.at[below])
    for i, source in enumerate(sources):
        copy = pltpu.make_async_copy(source, stage.at[i], sems.at[i])
        copy.wait() if wait else copy.start()


def first_kernel(ints, left, mps, psi, rights, stage, sems):
    @pl.when(ints[0] == 0)
    def _():
        fetch(0, left, mps, psi, rights, stage, sems, False)
        fetch(0, left, mps, psi, rights, stage, sems, True)


def sector_kernel(step, ints, floats, arrived, previous, stage, left, mps, psi, rights, *rest):
    environ, staged, keep, send, results, total, sems, stores = rest[-8:]
    site, my_z, my_x, core = ints[0], ints[1], ints[2], ints[3]
    q = step - LAG * site
    below = jnp.maximum(q - 1, 0)
    above = jnp.minimum(q + 1, NQ - 1)
    more = (q >= -1) & (q < NQ - 1) & (step < LAST - 1)

    @pl.when(more)
    def _():
        fetch(q + 1, left, mps, psi, rights, staged, sems, False)

    @pl.when((q >= 0) & (q < NQ))
    def _():
        size, under, over = ints[4 + q], ints[4 + below], ints[4 + above]
        present, present_above = ints[16 + q].astype(f32), ints[16 + above].astype(f32)
        present_above = jnp.where(q < NQ - 1, present_above, 0.0)
        c0 = jnp.where(site == 0, present, 1.0) * floats[0]
        c1 = jnp.where(site == 0, ints[16 + below].astype(f32), 1.0) * floats[1]
        now = jnp.where(site == 0, stage[0], arrived[...])
        before = jnp.where(site == 0, stage[7], previous[...])
        before = jnp.where(q > 0, before, 0.0)
        s = framed(stage[1], size, size)
        u = framed(stage[2], under, size)
        first = c0 * product(halves(now), halves(s), ((1,), (0,)))
        second = c1 * product(halves(before), halves(u), ((1,), (0,)))
        moved = product(halves(s.T), halves(first), ((1,), (0,))) + product(
            halves(u.T), halves(second), ((1,), (0,)))
        environ[...] = moved
        total[...] = moved

        def move(state, i, target, near, far, third):
            return pltpu.make_async_copy(
                results.at[state, pl.ds(ROWS * i, ROWS)], target.at[state, near, far, third], stores)

        def apply(state, _):
            c = jnp.where(state == 0, floats[2] * present, floats[3] * present_above)
            n = jnp.where(state == 0, size, over)
            part = c * product(halves(total[...]), halves(stage[3 + state]), ((1,), (0,)))
            results[state] = product(halves(part), halves(framed(stage[5 + state], n, n)), ((1,), (1,)))

            def place(i, _):
                piece = (W // ROWS) * q + i
                owner, third = piece // 3, piece % 3
                z = (owner // 8 - my_z + 4) % 4
                x = ((owner // 2) % 4 - my_x + 4) % 4
                near = jnp.where(state == 0, x, z)
                far = jnp.where(state == 0, z, x)
                mine = owner % 2 == core

                @pl.when(mine)
                def _():
                    move(state, i, keep, near, far, third).start()

                @pl.when(jnp.logical_not(mine))
                def _():
                    move(state, i, send, near, far, third).start()

                return 0

            return lax.fori_loop(0, W // ROWS, place, 0)

        lax.fori_loop(0, 2, apply, 0)
        pltpu.make_async_copy(results, stage.at[pl.ds(0, 2)], stores).wait()

    @pl.when(more)
    def _():
        fetch(q + 1, left, mps, psi, rights, staged, sems, True)


LAST = NQ + LAG * (SITES - 1)
SCALAR = pl.BlockSpec(memory_space=pltpu.SMEM)
LOCAL = pl.BlockSpec(memory_space=pltpu.VMEM)
FAR = pl.BlockSpec(memory_space=pltpu.HBM)
STAGE = jax.ShapeDtypeStruct((8, W, W), f32)
GRANT = pltpu.CompilerParams(vmem_limit_bytes=53 * 2**20)


def first_stage(ints, left, mps, psi, rights):
    return pl.pallas_call(
        first_kernel, in_specs=[SCALAR] + [FAR] * 4, out_specs=LOCAL, out_shape=STAGE,
        scratch_shapes=[pltpu.SemaphoreType.DMA((8,))], compiler_params=GRANT, name="first",
    )(ints, left, mps, psi, rights)


def sector_step(step, ints, floats, arrived, previous, stage, left, mps, psi, rights, held):
    shape = jax.ShapeDtypeStruct((2, 4, 4, 3, ROWS, W), f32)

    def kernel(*refs):
        sector_kernel(step, *refs)

    return pl.pallas_call(
        kernel,
        in_specs=[SCALAR] * 2 + [LOCAL] * 3 + [FAR] * (4 + len(held)),
        out_specs=[LOCAL, LOCAL, FAR, FAR],
        out_shape=[jax.ShapeDtypeStruct((W, W), f32), STAGE, shape, shape],
        scratch_shapes=[
            pltpu.VMEM((2, W, W), f32),
            pltpu.VMEM((W, W), f32),
            pltpu.SemaphoreType.DMA((8,)),
            pltpu.SemaphoreType.DMA,
        ],
        input_output_aliases={9: 2, 10: 3} if held else {},
        compiler_params=GRANT,
        name=f"sector{step}",
    )(ints, floats, arrived, previous, stage, left, mps, psi, rights, *held)


def turned(x, axis, by):
    return lax.ppermute(x, axis, [(i, (i + by) % 4) for i in range(4)])


def round_far(blocks, axis):
    half = blocks.shape[1] // 2
    up = turned(blocks[2, :half], axis, 1)
    down = turned(blocks[2, half:], axis, -1)
    return blocks[0], jnp.concatenate([blocks[1, :half] + up, blocks[1, half:]]), jnp.concatenate(
        [blocks[3, :half], blocks[3, half:] + down])


def round_near(parts, axis):
    own, ahead, behind = parts
    return own + turned(ahead, axis, 1) + turned(behind, axis, -1)


def reduced(keep, send):
    both = keep + lax.ppermute(send, "core", [(0, 1), (1, 0)])
    both = both.reshape(2, 4, 4, 96, W)
    first, second = round_far(both[0], "x"), round_far(both[1], "z")
    first, second = round_near(first, "x"), round_near(second, "z")
    first, second = round_far(first, "z"), round_far(second, "x")
    return jnp.stack([round_near(first, "z"), round_near(second, "x")])[None]


def shards(left_env, right_env, mps, psi, coef, sector_sizes, pattern):
    place = jnp.stack([lax.axis_index(a) for a in ("site", "z", "x", "core")]).astype(jnp.int32)
    ints = jnp.concatenate([place, sector_sizes, pattern[0]])
    floats = coef[0, 0]
    sources = (left_env[0], mps[0], psi[0], right_env[0, 0])
    nothing = jnp.zeros((W, W), f32)
    arrivals = {}
    held = ()
    stage = first_stage(ints, *sources)
    for step in range(LAST):
        arrived = arrivals.get(step, nothing)
        environ, stage, *held = sector_step(
            step, ints, floats, arrived, arrivals.get(step - 1, nothing), stage, *sources, tuple(held))
        if step + LAG < LAST:
            arrivals[step + LAG] = lax.ppermute(environ, "site", [(0, 1), (1, 2), (2, 3)])
    return reduced(*held)


def solution(mesh):
    fine = Mesh(mesh.devices.reshape(4, 4, 4, 2), ("site", "z", "x", "core"))
    term = ("z", "x", "core")
    return jax.shard_map(
        shards,
        mesh=fine,
        in_specs=(
            P(term, None, None, None),
            P("site", term, None, None, None),
            P("site", None, None, None, None),
            P("site", None, None, None, None),
            P("site", term, None),
            P(),
            P(term, None),
        ),
        out_specs=P("site", None, term, None),
        check_vma=False,
    )
```

```python
import jax
import jax.numpy as jnp
from jax import lax
from jax.experimental import pallas as pl
from jax.experimental.pallas import tpu as pltpu
from jax.sharding import Mesh, PartitionSpec as P

f32, bf16 = jnp.float32, jnp.bfloat16
W = 256
NQ = 12
ROWS = 32
SITES = 4
LAG = 2


def halves(x):
    high = x.astype(bf16)
    return high, (x - high.astype(f32)).astype(bf16)


def product(a, b, dims):
    (ah, al), (bh, bl) = a, b

    def dot(u, v):
        return lax.dot_general(u, v, (dims, ((), ())), preferred_element_type=f32)

    return dot(ah, bh) + (dot(ah, bl) + dot(al, bh))


def framed(x, rows, columns):
    i = lax.broadcasted_iota(jnp.int32, x.shape, 0)
    j = lax.broadcasted_iota(jnp.int32, x.shape, 1)
    return jnp.where((i < rows) & (j < columns), x, 0.0)


def sector_kernel(step, ints, floats, arrived, previous, left, mps, psi, rights, *rest):
    environ, keep, send, results, total, stores = rest[-6:]
    site, my_z, my_x, core = ints[0], ints[1], ints[2], ints[3]
    q = step - LAG * site
    below = jnp.maximum(q - 1, 0)
    above = jnp.minimum(q + 1, NQ - 1)
    @pl.when((q >= 0) & (q < NQ))
    def _():
        size, under, over = ints[4 + q], ints[4 + below], ints[4 + above]
        present, present_above = ints[16 + q].astype(f32), ints[16 + above].astype(f32)
        present_above = jnp.where(q < NQ - 1, present_above, 0.0)
        c0 = jnp.where(site == 0, present, 1.0) * floats[0]
        c1 = jnp.where(site == 0, ints[16 + below].astype(f32), 1.0) * floats[1]
        now = jnp.where(site == 0, left[q], arrived[...])
        before = jnp.where(site == 0, left[below], previous[...])
        before = jnp.where(q > 0, before, 0.0)
        s = framed(mps[0, q], size, size)
        u = framed(mps[1, below], under, size)
        first = c0 * product(halves(now), halves(s), ((1,), (0,)))
        second = c1 * product(halves(before), halves(u), ((1,), (0,)))
        moved = product(halves(s.T), halves(first), ((1,), (0,))) + product(
            halves(u.T), halves(second), ((1,), (0,)))
        environ[...] = moved
        total[...] = moved

        def move(state, i, target, near, far, third):
            return pltpu.make_async_copy(
                results.at[state, pl.ds(ROWS * i, ROWS)], target.at[state, near, far, third], stores)

        def apply(state, _):
            c = jnp.where(state == 0, floats[2] * present, floats[3] * present_above)
            n = jnp.where(state == 0, size, over)
            part = c * product(halves(total[...]), halves(psi[state, q]), ((1,), (0,)))
            results[state] = product(halves(part), halves(framed(rights[jnp.where(state == 0, q, above)], n, n)), ((1,), (1,)))

            def place(i, _):
                piece = (W // ROWS) * q + i
                owner, third = piece // 3, piece % 3
                z = (owner // 8 - my_z + 4) % 4
                x = ((owner // 2) % 4 - my_x + 4) % 4
                near = jnp.where(state == 0, x, z)
                far = jnp.where(state == 0, z, x)
                mine = owner % 2 == core

                @pl.when(mine)
                def _():
                    move(state, i, keep, near, far, third).start()

                @pl.when(jnp.logical_not(mine))
                def _():
                    move(state, i, send, near, far, third).start()

                return 0

            return lax.fori_loop(0, W // ROWS, place, 0)

        lax.fori_loop(0, 2, apply, 0)
        pltpu.make_async_copy(results, psi.at[:, 0], stores).wait()


LAST = NQ + LAG * (SITES - 1)
SCALAR = pl.BlockSpec(memory_space=pltpu.SMEM)
LOCAL = pl.BlockSpec(memory_space=pltpu.VMEM)
FAR = pl.BlockSpec(memory_space=pltpu.HBM)
GRANT = pltpu.CompilerParams(vmem_limit_bytes=8 * 2**20)


def sector_step(step, ints, floats, arrived, previous, left, mps, psi, rights, held):
    shape = jax.ShapeDtypeStruct((2, 4, 4, 3, ROWS, W), f32)

    def kernel(*refs):
        sector_kernel(step, *refs)

    return pl.pallas_call(
        kernel,
        in_specs=[SCALAR] * 2 + [LOCAL] * 6 + [FAR] * len(held),
        out_specs=[LOCAL, FAR, FAR],
        out_shape=[jax.ShapeDtypeStruct((W, W), f32), shape, shape],
        scratch_shapes=[
            pltpu.VMEM((2, W, W), f32),
            pltpu.VMEM((W, W), f32),
            pltpu.SemaphoreType.DMA,
        ],
        input_output_aliases={8: 1, 9: 2} if held else {},
        compiler_params=GRANT,
        name=f"sector{step}",
    )(ints, floats, arrived, previous, left, mps, psi, rights, *held)


def turned(x, axis, by):
    return lax.ppermute(x, axis, [(i, (i + by) % 4) for i in range(4)])


def round_far(blocks, axis):
    half = blocks.shape[1] // 2
    up = turned(blocks[2, :half], axis, 1)
    down = turned(blocks[2, half:], axis, -1)
    return blocks[0], jnp.concatenate([blocks[1, :half] + up, blocks[1, half:]]), jnp.concatenate(
        [blocks[3, :half], blocks[3, half:] + down])


def round_near(parts, axis):
    own, ahead, behind = parts
    return own + turned(ahead, axis, 1) + turned(behind, axis, -1)


def reduced(keep, send):
    both = keep + lax.ppermute(send, "core", [(0, 1), (1, 0)])
    both = both.reshape(2, 4, 4, 96, W)
    first, second = round_far(both[0], "x"), round_far(both[1], "z")
    first, second = round_near(first, "x"), round_near(second, "z")
    first, second = round_far(first, "z"), round_far(second, "x")
    return jnp.stack([round_near(first, "z"), round_near(second, "x")])[None]


def shards(left_env, right_env, mps, psi, coef, sector_sizes, pattern):
    place = jnp.stack([lax.axis_index(a) for a in ("site", "z", "x", "core")]).astype(jnp.int32)
    ints = jnp.concatenate([place, sector_sizes, pattern[0]])
    floats = coef[0, 0]
    sources = (left_env[0], mps[0], psi[0], right_env[0, 0])
    nothing = jnp.zeros((W, W), f32)
    arrivals = {}
    held = ()
    for step in range(LAST):
        arrived = arrivals.get(step, nothing)
        environ, *held = sector_step(
            step, ints, floats, arrived, arrivals.get(step - 1, nothing), *sources, tuple(held))
        if step + LAG < LAST:
            arrivals[step + LAG] = lax.ppermute(environ, "site", [(0, 1), (1, 2), (2, 3)])
    return reduced(*held)


def solution(mesh):
    fine = Mesh(mesh.devices.reshape(4, 4, 4, 2), ("site", "z", "x", "core"))
    term = ("z", "x", "core")
    return jax.shard_map(
        shards,
        mesh=fine,
        in_specs=(
            P(term, None, None, None),
            P("site", term, None, None, None),
            P("site", None, None, None, None),
            P("site", None, None, None, None),
            P("site", term, None),
            P(),
            P(term, None),
        ),
        out_specs=P("site", None, term, None),
        check_vma=False,
    )
```

```python
import jax
import jax.numpy as jnp
from jax import lax
from jax.experimental import pallas as pl
from jax.experimental.pallas import tpu as pltpu
from jax.sharding import Mesh, PartitionSpec as P

f32, bf16 = jnp.float32, jnp.bfloat16
W = 256
NQ = 12
ROWS = 32
SITES = 4
LAG = 2


def halves(x):
    high = x.astype(bf16)
    return high, (x - high.astype(f32)).astype(bf16)


def product(a, b, dims):
    (ah, al), (bh, bl) = a, b

    def dot(u, v):
        return lax.dot_general(u, v, (dims, ((), ())), preferred_element_type=f32)

    return dot(ah, bh) + (dot(ah, bl) + dot(al, bh))


def framed(x, rows, columns):
    i = lax.broadcasted_iota(jnp.int32, x.shape, 0)
    j = lax.broadcasted_iota(jnp.int32, x.shape, 1)
    return jnp.where((i < rows) & (j < columns), x, 0.0)


def sector_kernel(step, ints, floats, arrived, previous, left, mps, psi, rights, *rest):
    environ, keep, send_far, send_rest, results, total, stores = rest[-7:]
    site, my_z, my_x, core = ints[0], ints[1], ints[2], ints[3]
    q = step - LAG * site
    below = jnp.maximum(q - 1, 0)
    above = jnp.minimum(q + 1, NQ - 1)
    @pl.when((q >= 0) & (q < NQ))
    def _():
        size, under, over = ints[4 + q], ints[4 + below], ints[4 + above]
        present, present_above = ints[16 + q].astype(f32), ints[16 + above].astype(f32)
        present_above = jnp.where(q < NQ - 1, present_above, 0.0)
        c0 = jnp.where(site == 0, present, 1.0) * floats[0]
        c1 = jnp.where(site == 0, ints[16 + below].astype(f32), 1.0) * floats[1]
        now = jnp.where(site == 0, left[q], arrived[...])
        before = jnp.where(site == 0, left[below], previous[...])
        before = jnp.where(q > 0, before, 0.0)
        s = framed(mps[0, q], size, size)
        u = framed(mps[1, below], under, size)
        s, u = halves(s.T), halves(u.T)
        first = c0 * product(halves(now), s, ((1,), (1,)))
        second = c1 * product(halves(before), u, ((1,), (1,)))
        moved = product(s, halves(first), ((1,), (0,))) + product(u, halves(second), ((1,), (0,)))
        environ[...] = moved
        total[...] = moved

        def move(state, i, target):
            return pltpu.make_async_copy(results.at[state, pl.ds(ROWS * i, ROWS)], target, stores)

        def apply(state, _):
            c = jnp.where(state == 0, floats[2] * present, floats[3] * present_above)
            n = jnp.where(state == 0, size, over)
            part = c * product(halves(total[...]), halves(psi[state, q]), ((1,), (0,)))
            results[state] = product(halves(part), halves(framed(rights[jnp.where(state == 0, q, above)], n, n)), ((1,), (1,)))

            def place(i, _):
                piece = (W // ROWS) * q + i
                owner, third = piece // 3, piece % 3
                z = (owner // 8 - my_z + 4) % 4
                x = ((owner // 2) % 4 - my_x + 4) % 4
                near = jnp.where(state == 0, x, z)
                far = jnp.where(state == 0, z, x)
                mine = owner % 2 == core

                @pl.when(mine)
                def _():
                    move(state, i, keep.at[state, near, far, third]).start()

                @pl.when(jnp.logical_not(mine) & (near == 2))
                def _():
                    move(state, i, send_far.at[state, far, third]).start()

                @pl.when(jnp.logical_not(mine) & (near != 2))
                def _():
                    move(state, i, send_rest.at[state, jnp.minimum(near, 2), far, third]).start()

                return 0

            return lax.fori_loop(0, W // ROWS, place, 0)

        lax.fori_loop(0, 2, apply, 0)
        pltpu.make_async_copy(results, psi.at[:, 0], stores).wait()


LAST = NQ + LAG * (SITES - 1)
SCALAR = pl.BlockSpec(memory_space=pltpu.SMEM)
LOCAL = pl.BlockSpec(memory_space=pltpu.VMEM)
FAR = pl.BlockSpec(memory_space=pltpu.HBM)
GRANT = pltpu.CompilerParams(vmem_limit_bytes=8 * 2**20)


def sector_step(step, ints, floats, arrived, previous, left, mps, psi, rights, held):
    shapes = [jax.ShapeDtypeStruct(s + (3, ROWS, W), f32) for s in ((2, 4, 4), (2, 4), (2, 3, 4))]

    def kernel(*refs):
        sector_kernel(step, *refs)

    return pl.pallas_call(
        kernel,
        in_specs=[SCALAR] * 2 + [LOCAL] * 6 + [FAR] * len(held),
        out_specs=[LOCAL] + [FAR] * 3,
        out_shape=[jax.ShapeDtypeStruct((W, W), f32)] + shapes,
        scratch_shapes=[
            pltpu.VMEM((2, W, W), f32),
            pltpu.VMEM((W, W), f32),
            pltpu.SemaphoreType.DMA,
        ],
        input_output_aliases={8: 1, 9: 2, 10: 3} if held else {},
        compiler_params=GRANT,
        name=f"sector{step}",
    )(ints, floats, arrived, previous, left, mps, psi, rights, *held)


def turned(x, axis, by):
    return lax.ppermute(x, axis, [(i, (i + by) % 4) for i in range(4)])


def swapped(x):
    return lax.ppermute(x, "core", [(0, 1), (1, 0)])


def first_phase(far, own, ahead, behind, axis):
    up = turned(far[:2], axis, 1)
    down = turned(far[2:], axis, -1)
    ahead = jnp.concatenate([ahead[:2] + up, ahead[2:]])
    behind = jnp.concatenate([behind[:2], behind[2:] + down])
    return own + turned(ahead, axis, 1) + turned(behind, axis, -1)


def second_phase(blocks, axis):
    return (blocks[0] + turned(blocks[1], axis, 1)) + (turned(blocks[3], axis, -1) + turned(blocks[2], axis, 2))


def reduced(keep, send_far, send_rest):
    far = (keep[:, 2] + swapped(send_far)).reshape(2, 4, 96, W)
    rest = swapped(send_rest)
    own, ahead, behind = [
        (keep[:, i] + rest[:, j]).reshape(2, 4, 96, W) for i, j in ((0, 0), (1, 1), (3, 2))]
    first = first_phase(far[0], own[0], ahead[0], behind[0], "x")
    second = first_phase(far[1], own[1], ahead[1], behind[1], "z")
    return jnp.stack([second_phase(first, "z"), second_phase(second, "x")])[None]


def shards(left_env, right_env, mps, psi, coef, sector_sizes, pattern):
    place = jnp.stack([lax.axis_index(a) for a in ("site", "z", "x", "core")]).astype(jnp.int32)
    ints = jnp.concatenate([place, sector_sizes, pattern[0]])
    floats = coef[0, 0]
    sources = (left_env[0], mps[0], psi[0], right_env[0, 0])
    starts = (left_env[0, :LAG], mps[0, :, :LAG], psi[0, :, :LAG], right_env[0, 0, : LAG + 1])
    nothing = jnp.zeros((W, W), f32)
    arrivals = {}
    held = ()
    for step in range(LAST):
        arrived = arrivals.get(step, nothing)
        environ, *held = sector_step(
            step, ints, floats, arrived, arrivals.get(step - 1, nothing), *(starts if step < LAG else sources), tuple(held))
        if step + LAG < LAST:
            arrivals[step + LAG] = lax.ppermute(environ, "site", [(0, 1), (1, 2), (2, 3)])
    return reduced(*held)


def solution(mesh):
    fine = Mesh(mesh.devices.reshape(4, 4, 4, 2), ("site", "z", "x", "core"))
    term = ("z", "x", "core")
    return jax.shard_map(
        shards,
        mesh=fine,
        in_specs=(
            P(term, None, None, None),
            P("site", term, None, None, None),
            P("site", None, None, None, None),
            P("site", None, None, None, None),
            P("site", term, None),
            P(),
            P(term, None),
        ),
        out_specs=P("site", None, term, None),
        check_vma=False,
    )
```

```python
import jax
import jax.numpy as jnp
from jax import lax
from jax.experimental import pallas as pl
from jax.experimental.pallas import tpu as pltpu
from jax.sharding import Mesh, PartitionSpec as P

f32, bf16 = jnp.float32, jnp.bfloat16
W = 256
NQ = 12
ROWS = 32
SITES = 4
LAG = 2


def halves(x):
    high = x.astype(bf16)
    return high, (x - high.astype(f32)).astype(bf16)


def product(a, b, dims):
    (ah, al), (bh, bl) = a, b

    def dot(u, v):
        return lax.dot_general(u, v, (dims, ((), ())), preferred_element_type=f32)

    return dot(ah, bh) + (dot(ah, bl) + dot(al, bh))


def framed(x, rows, columns):
    i = lax.broadcasted_iota(jnp.int32, x.shape, 0)
    j = lax.broadcasted_iota(jnp.int32, x.shape, 1)
    return jnp.where((i < rows) & (j < columns), x, 0.0)


LAST = NQ + LAG * (SITES - 1)
SCALAR = pl.BlockSpec(memory_space=pltpu.SMEM)
LOCAL = pl.BlockSpec(memory_space=pltpu.VMEM)
FAR = pl.BlockSpec(memory_space=pltpu.HBM)
GRANT = pltpu.CompilerParams(vmem_limit_bytes=8 * 2**20)
BUFFER = jax.ShapeDtypeStruct((4, 4, 2, 3, ROWS, W), f32)


def update_part(q, ints, floats, arrived, previous, left, mps):
    site = ints[0]
    below = jnp.maximum(q - 1, 0)
    size, under = ints[4 + q], ints[4 + below]
    c0 = jnp.where(site == 0, ints[16 + q].astype(f32), 1.0) * floats[0]
    c1 = jnp.where(site == 0, ints[16 + below].astype(f32), 1.0) * floats[1]
    now = jnp.where(site == 0, left[q], arrived[...])
    before = jnp.where(site == 0, left[below], previous[...])
    before = jnp.where(q > 0, before, 0.0)
    s = framed(mps[0, q], size, size)
    u = framed(mps[1, below], under, size)
    first = c0 * product(halves(now), halves(s), ((1,), (0,)))
    second = c1 * product(halves(before), halves(u), ((1,), (0,)))
    return product(halves(s.T), halves(first), ((1,), (0,))) + product(
        halves(u.T), halves(second), ((1,), (0,)))


def apply_part(q, ints, floats, psi, rights, keep, send, results, total, stores):
    my_z, my_x, core = ints[1], ints[2], ints[3]
    above = jnp.minimum(q + 1, NQ - 1)
    present_above = jnp.where(q < NQ - 1, ints[16 + above], 0)

    def one_state(state, _):
        other = jnp.where(state == 0, q, above)
        present = jnp.where(state == 0, ints[16 + q], present_above)
        c = floats[2 + state] * present.astype(f32)
        n = ints[4 + other]
        part = c * product(halves(total[...]), halves(psi[state, q]), ((1,), (0,)))
        results[state] = product(halves(part), halves(framed(rights[other], n, n)), ((1,), (1,)))

        def place(target):
            for i in range(W // ROWS):
                piece = (W // ROWS) * q + i
                owner, third = piece // 3, piece % 3
                z = (owner // 8 - my_z + 4) % 4
                x = ((owner // 2) % 4 - my_x + 4) % 4
                near, far = jnp.where(state == 0, x, z), jnp.where(state == 0, z, x)
                pltpu.make_async_copy(
                    results.at[state, pl.ds(ROWS * i, ROWS)], target.at[near, far, owner % 2, third], stores).start()

        @pl.when(state == core)
        def _():
            place(keep)

        @pl.when(state != core)
        def _():
            place(send)

        return 0

    lax.fori_loop(0, 2, one_state, 0)
    pltpu.make_async_copy(results, psi.at[:, 0], stores).wait()


def sector_step(step, ints, floats, arrived, previous, left, mps, psi, rights, saved, held):
    sending, applying = step + LAG < LAST, step >= LAG
    late = NQ <= step < NQ + LAG
    n_in = 6 + (2 if applying else 0) + (1 if late else 0)

    def kernel(*refs):
        ints, floats, arrived, previous, left, mps = refs[:6]
        outs = refs[n_in + len(held):]
        environ = outs[0] if sending else None
        q = step - LAG * ints[0]
        active = (q >= 0) & (q < NQ)
        total = outs[-2] if applying else None

        @pl.when(active)
        def _():
            moved = update_part(q, ints, floats, arrived, previous, left, mps)
            if sending:
                environ[...] = moved
            if applying:
                total[...] = moved

        if applying:
            psi, rights = refs[6:8]
            keep, send = outs[1:3] if sending else outs[:2]
            if late:
                @pl.when(ints[0] == 0)
                def _():
                    total[...] = refs[8][...]

                active = active | (ints[0] == 0)
                q = jnp.where(ints[0] == 0, step - NQ, q)

            @pl.when(active)
            def _():
                apply_part(q, ints, floats, psi, rights, keep, send, *outs[-3:])

    operands = (arrived, previous, left, mps) + ((psi, rights) if applying else ()) + ((saved,) if late else ())
    first_out = 1 if sending else 0
    return pl.pallas_call(
        kernel,
        in_specs=[SCALAR] * 2 + [LOCAL] * len(operands) + [FAR] * len(held),
        out_specs=[LOCAL] * first_out + ([FAR] * 2 if applying else []),
        out_shape=[jax.ShapeDtypeStruct((W, W), f32)] * first_out + ([BUFFER] * 2 if applying else []),
        scratch_shapes=[
            pltpu.VMEM((2, W, W), f32),
            pltpu.VMEM((W, W), f32),
            pltpu.SemaphoreType.DMA,
        ] if applying else [],
        input_output_aliases={n_in + i: first_out + i for i in range(len(held))},
        compiler_params=GRANT,
        name=f"sector{step}",
    )(ints, floats, *operands, *held)


TERM = ("z", "x", "core")


def swapped(x):
    return lax.ppermute(x, "core", [(0, 1), (1, 0)])


def turned(x, first, by):
    pairs = []
    for z in range(4):
        for x_ in range(4):
            for c in range(2):
                along_x = (c == 0) == first
                to = (z, (x_ + by) % 4) if along_x else ((z + by) % 4, x_)
                pairs.append((8 * z + 2 * x_ + c, 8 * to[0] + 2 * to[1] + c))
    return lax.ppermute(x, TERM, pairs)


def reduced(keep, send, core):
    both = (keep + swapped(send)).reshape(4, 4, 192, W)
    up = turned(both[2, :2], True, 1)
    down = turned(both[2, 2:], True, -1)
    ahead = jnp.concatenate([both[1, :2] + up, both[1, 2:]])
    behind = jnp.concatenate([both[3, :2], both[3, 2:] + down])
    line = both[0] + turned(ahead, True, 1) + turned(behind, True, -1)
    rows = (line[0] + turned(line[1], False, 1)) + (turned(line[3], False, -1) + turned(line[2], False, 2))
    rows = rows.reshape(2, 96, W)
    mine = jnp.where(core == 0, rows[0], rows[1])
    got = swapped(jnp.where(core == 0, rows[1], rows[0]))
    return jnp.stack([jnp.where(core == 0, mine, got), jnp.where(core == 0, got, mine)])[None]


def shards(left_env, right_env, mps, psi, coef, sector_sizes, pattern):
    place = jnp.stack([lax.axis_index(a) for a in ("site",) + TERM]).astype(jnp.int32)
    ints = jnp.concatenate([place, sector_sizes, pattern[0]])
    floats = coef[0, 0]
    sources = (left_env[0], mps[0], psi[0], right_env[0, 0])
    nothing = jnp.zeros((W, W), f32)
    arrivals, environs, held = {}, {}, ()
    for step in range(LAST):
        out = sector_step(
            step, ints, floats, arrivals.get(step, nothing), arrivals.get(step - 1, nothing), *sources,
            environs.get(step - NQ), held)
        if step + LAG < LAST:
            environs[step], *out = out
            arrivals[step + LAG] = lax.ppermute(environs[step], "site", [(0, 1), (1, 2), (2, 3)])
        held = tuple(out)
    return reduced(*held, place[3])


def solution(mesh):
    fine = Mesh(mesh.devices.reshape(4, 4, 4, 2), ("site", "z", "x", "core"))
    term = ("z", "x", "core")
    return jax.shard_map(
        shards,
        mesh=fine,
        in_specs=(
            P(term, None, None, None),
            P("site", term, None, None, None),
            P("site", None, None, None, None),
            P("site", None, None, None, None),
            P("site", term, None),
            P(),
            P(term, None),
        ),
        out_specs=P("site", None, term, None),
        check_vma=False,
    )
```

```python
import jax
import jax.numpy as jnp
from jax import lax
from jax.experimental import pallas as pl
from jax.experimental.pallas import tpu as pltpu
from jax.sharding import Mesh, PartitionSpec as P

f32, bf16 = jnp.float32, jnp.bfloat16
W = 256
NQ = 12
ROWS = 32
SITES = 4
LAG = 2


def halves(x):
    high = x.astype(bf16)
    return high, (x - high.astype(f32)).astype(bf16)


def product(a, b, dims):
    (ah, al), (bh, bl) = a, b

    def dot(u, v):
        return lax.dot_general(u, v, (dims, ((), ())), preferred_element_type=f32)

    return dot(ah, bh) + (dot(ah, bl) + dot(al, bh))


def framed(x, rows, columns):
    i = lax.broadcasted_iota(jnp.int32, x.shape, 0)
    j = lax.broadcasted_iota(jnp.int32, x.shape, 1)
    return jnp.where((i < rows) & (j < columns), x, 0.0)


LAST = NQ + LAG * (SITES - 1)
SCALAR = pl.BlockSpec(memory_space=pltpu.SMEM)
LOCAL = pl.BlockSpec(memory_space=pltpu.VMEM)
FAR = pl.BlockSpec(memory_space=pltpu.HBM)
GRANT = pltpu.CompilerParams(vmem_limit_bytes=8 * 2**20)
BUFFER = jax.ShapeDtypeStruct((2, 2, 4, 4, 3, ROWS, W), f32)


def update_part(q, ints, floats, arrived, previous, left, mps):
    site = ints[0]
    below = jnp.maximum(q - 1, 0)
    size, under = ints[4 + q], ints[4 + below]
    c0 = jnp.where(site == 0, ints[16 + q].astype(f32), 1.0) * floats[0]
    c1 = jnp.where(site == 0, ints[16 + below].astype(f32), 1.0) * floats[1]
    now = jnp.where(site == 0, left[q], arrived[...])
    before = jnp.where(site == 0, left[below], previous[...])
    before = jnp.where(q > 0, before, 0.0)
    s = framed(mps[0, q], size, size)
    u = framed(mps[1, below], under, size)
    first = c0 * product(halves(now), halves(s), ((1,), (0,)))
    second = c1 * product(halves(before), halves(u), ((1,), (0,)))
    return product(halves(s.T), halves(first), ((1,), (0,))) + product(
        halves(u.T), halves(second), ((1,), (0,)))


def apply_part(q, e, ints, floats, psi, rights, pieces, results, stores):
    my_z, my_x, core = ints[1], ints[2], ints[3]
    above = jnp.minimum(q + 1, NQ - 1)
    e = halves(e)
    present = ints[16 + q].astype(f32)
    present_above = jnp.where(q < NQ - 1, ints[16 + above], 0).astype(f32)

    def one_state(state, _):
        other = jnp.where(state == 0, q, above)
        c = jnp.where(state == 0, floats[2] * present, floats[3] * present_above)
        n = ints[4 + other]
        part = c * product(e, halves(psi[state, q]), ((1,), (0,)))
        results[state] = product(halves(part), halves(framed(rights[other], n, n)), ((1,), (1,)))
        for i in range(W // ROWS):
            piece = (W // ROWS) * q + i
            owner, third = piece // 3, piece % 3
            z = (owner // 8 - my_z + 4) % 4
            x = ((owner // 2) % 4 - my_x + 4) % 4
            sent = (owner + core) % 2
            near, far = jnp.where(state == 0, x, z), jnp.where(state == 0, z, x)
            pltpu.make_async_copy(
                results.at[state, pl.ds(ROWS * i, ROWS)], pieces.at[sent, state, near, far, third], stores).start()
        return 0

    lax.fori_loop(0, 2, one_state, 0)
    pltpu.make_async_copy(results, psi.at[:, 0], stores).wait()


def update_step(step, ints, floats, arrived, previous, left, mps, held):
    def kernel(ints, floats, arrived, previous, left, mps, *rest):
        environ = rest[-1]
        q = step - LAG * ints[0]

        @pl.when((q >= 0) & (q < NQ))
        def _():
            environ[...] = update_part(q, ints, floats, arrived, previous, left, mps)

    return pl.pallas_call(
        kernel, in_specs=[SCALAR] * 2 + [LOCAL] * 4 + [FAR] * len(held), out_specs=LOCAL, out_shape=jax.ShapeDtypeStruct((W, W), f32),
        compiler_params=GRANT, name=f"update{step}",
    )(ints, floats, arrived, previous, left, mps, *held)


def apply_step(step, ints, floats, environ, psi, rights, saved, held):
    late = NQ <= step < NQ + LAG
    operands = (environ, psi, rights) + ((saved,) if late else ())

    def kernel(*refs):
        ints, floats, environ, psi, rights = refs[:5]
        q = step - LAG * ints[0]
        active = (q >= 0) & (q < NQ)
        first = ints[0] == 0
        if late:
            active = active | first
            q = jnp.where(first, step - NQ, q)

        @pl.when(active)
        def _():
            e = environ[...]
            if late:
                e = jnp.where(first, refs[5][...], e)
            apply_part(q, e, ints, floats, psi, rights, *refs[-3:])

    return pl.pallas_call(
        kernel,
        in_specs=[SCALAR] * 2 + [LOCAL] * len(operands) + [FAR] * len(held),
        out_specs=[FAR],
        out_shape=[BUFFER],
        scratch_shapes=[pltpu.VMEM((2, W, W), f32), pltpu.SemaphoreType.DMA],
        input_output_aliases={2 + len(operands): 0} if held else {},
        compiler_params=GRANT,
        name=f"apply{step}",
    )(ints, floats, *operands, *held)


def turned(x, axis, by):
    return lax.ppermute(x, axis, [(i, (i + by) % 4) for i in range(4)])


def first_phase(both, axis):
    up = turned(both[2, :2], axis, 1)
    down = turned(both[2, 2:], axis, -1)
    ahead = jnp.concatenate([both[1, :2] + up, both[1, 2:]])
    behind = jnp.concatenate([both[3, :2], both[3, 2:] + down])
    return both[0] + turned(ahead, axis, 1) + turned(behind, axis, -1)


def second_phase(line, axis):
    return (line[0] + turned(line[1], axis, 1)) + (turned(line[3], axis, -1) + turned(line[2], axis, 2))


def reduced(pieces):
    both = pieces[0] + lax.ppermute(pieces[1], "core", [(0, 1), (1, 0)])
    both = both.reshape(2, 4, 4, 96, W)
    first = first_phase(both[0], "x")
    second = first_phase(both[1], "z")
    return jnp.stack([second_phase(first, "z"), second_phase(second, "x")])[None]


TERM = ("z", "x", "core")


def shards(left_env, right_env, mps, psi, coef, sector_sizes, pattern):
    place = jnp.stack([lax.axis_index(a) for a in ("site",) + TERM]).astype(jnp.int32)
    ints = jnp.concatenate([place, sector_sizes, pattern[0]])
    floats = coef[0, 0]
    nothing = jnp.zeros((W, W), f32)
    arrivals, environs, held = {}, {}, ()
    for step in range(LAST):
        environ = update_step(
            step, ints, floats, arrivals.get(step, nothing), arrivals.get(step - 1, nothing), left_env[0], mps[0], held)
        environs[step] = environ
        if step + LAG < LAST:
            arrivals[step + LAG] = lax.ppermute(environ, "site", [(0, 1), (1, 2), (2, 3)])
        if step >= LAG:
            held = apply_step(step, ints, floats, environ, psi[0], right_env[0, 0], environs.get(step - NQ), held)
    return reduced(*held)


def solution(mesh):
    fine = Mesh(mesh.devices.reshape(4, 4, 4, 2), ("site", "z", "x", "core"))
    term = ("z", "x", "core")
    return jax.shard_map(
        shards,
        mesh=fine,
        in_specs=(
            P(term, None, None, None),
            P("site", term, None, None, None),
            P("site", None, None, None, None),
            P("site", None, None, None, None),
            P("site", term, None),
            P(),
            P(term, None),
        ),
        out_specs=P("site", None, term, None),
        check_vma=False,
    )
```

```python
import jax
import jax.numpy as jnp
from jax import lax
from jax.experimental import pallas as pl
from jax.experimental.pallas import tpu as pltpu
from jax.sharding import Mesh, PartitionSpec as P


f32, bf16 = jnp.float32, jnp.bfloat16
W = 256
NQ = 12
ROWS = 32
SITES = 4
LAG = 2


def halves(x):
    high = x.astype(bf16)
    return high, (x - high.astype(f32)).astype(bf16)


def product(a, b, dims):
    (ah, al), (bh, bl) = a, b

    def dot(u, v):
        return lax.dot_general(u, v, (dims, ((), ())), preferred_element_type=f32)

    return dot(ah, bh) + (dot(ah, bl) + dot(al, bh))


def framed(x, rows, columns):
    i = lax.broadcasted_iota(jnp.int32, x.shape, 0)
    j = lax.broadcasted_iota(jnp.int32, x.shape, 1)
    return jnp.where((i < rows) & (j < columns), x, 0.0)


LAST = NQ + LAG * (SITES - 1)
SCALAR = pl.BlockSpec(memory_space=pltpu.SMEM)
LOCAL = pl.BlockSpec(memory_space=pltpu.VMEM)
FAR = pl.BlockSpec(memory_space=pltpu.HBM)
GRANT = pltpu.CompilerParams(vmem_limit_bytes=8 * 2**20)
BUFFER = jax.ShapeDtypeStruct((2, 2, 4, 4, 3, ROWS, W), f32)


def update_part(q, ints, floats, arrived, previous, left, mps):
    site = ints[0]
    below = jnp.maximum(q - 1, 0)
    size, under = ints[4 + q], ints[4 + below]
    c0 = jnp.where(site == 0, ints[16 + q].astype(f32), 1.0) * floats[0]
    c1 = jnp.where(site == 0, ints[16 + below].astype(f32), 1.0) * floats[1]
    now = jnp.where(site == 0, left[q], arrived[...])
    before = jnp.where(site == 0, left[below], previous[...])
    before = jnp.where(q > 0, before, 0.0)
    s = framed(mps[0, q], size, size)
    u = framed(mps[1, below], under, size)
    first = c0 * product(halves(now), halves(s), ((1,), (0,)))
    second = c1 * product(halves(before), halves(u), ((1,), (0,)))
    return product(halves(s.T), halves(first), ((1,), (0,))) + product(
        halves(u.T), halves(second), ((1,), (0,)))


def apply_part(q, ints, floats, environs, psi, rights, pieces, results, stores):
    site, my_z, my_x, core = ints[0], ints[1], ints[2], ints[3]
    e = environs[0][...]
    for k in range(1, SITES):
        e = jnp.where(site == k, environs[k][...], e)
    e = halves(e)
    scales = [floats[2] * ints[16 + q].astype(f32)]
    if q < NQ - 1:
        scales.append(floats[3] * ints[17 + q].astype(f32))
    for state in range(2):
        if q + state < NQ:
            n = ints[4 + q + state]
            part = scales[state] * product(e, halves(psi[state, q]), ((1,), (0,)))
            results[state] = product(halves(part), halves(framed(rights[q + state], n, n)), ((1,), (1,)))
        else:
            results[state] = jnp.zeros((W, W), f32)
        for i in range(W // ROWS):
            owner, third = divmod((W // ROWS) * q + i, 3)
            z = (owner // 8 - my_z + 4) % 4
            x = ((owner // 2) % 4 - my_x + 4) % 4
            sent = core if owner % 2 == 0 else 1 - core
            near, far = ((x, z), (z, x))[state]
            pltpu.make_async_copy(
                results.at[state, pl.ds(ROWS * i, ROWS)], pieces.at[sent, state, near, far, third], stores).start()
    pltpu.make_async_copy(results, psi.at[:, 0], stores).wait()


def update_step(step, ints, floats, arrived, previous, left, mps, held):
    def kernel(ints, floats, arrived, previous, left, mps, *rest):
        environ = rest[-1]
        q = step - LAG * ints[0]

        @pl.when((q >= 0) & (q < NQ))
        def _():
            environ[...] = update_part(q, ints, floats, arrived, previous, left, mps)

    return pl.pallas_call(
        kernel, in_specs=[SCALAR] * 2 + [LOCAL] * 4 + [FAR] * len(held), out_specs=LOCAL, out_shape=jax.ShapeDtypeStruct((W, W), f32),
        compiler_params=GRANT,
    )(ints, floats, arrived, previous, left, mps, *held)


def apply_step(q, ints, floats, environs, psi, rights, held):
    def kernel(ints, floats, *refs):
        psi, rights = refs[SITES:SITES + 2]
        apply_part(q, ints, floats, refs[:SITES], psi, rights, *refs[-3:])

    operands = (*environs, psi, rights)
    return pl.pallas_call(
        kernel,
        in_specs=[SCALAR] * 2 + [LOCAL] * len(operands) + [FAR] * len(held),
        out_specs=[FAR],
        out_shape=[BUFFER],
        scratch_shapes=[pltpu.VMEM((2, W, W), f32), pltpu.SemaphoreType.DMA],
        input_output_aliases={2 + len(operands): 0} if held else {},
        compiler_params=GRANT,
    )(ints, floats, *operands, *held)


def turned(x, axis, by):
    return lax.ppermute(x, axis, [(i, (i + by) % 4) for i in range(4)])


def first_phase(both, axis):
    up = turned(both[2, :2], axis, 1)
    down = turned(both[2, 2:], axis, -1)
    ahead = jnp.concatenate([both[1, :2] + up, both[1, 2:]])
    behind = jnp.concatenate([both[3, :2], both[3, 2:] + down])
    return both[0] + turned(ahead, axis, 1) + turned(behind, axis, -1)


def second_phase(line, axis):
    return (line[0] + turned(line[1], axis, 1)) + (turned(line[3], axis, -1) + turned(line[2], axis, 2))


def reduced(pieces):
    both = pieces[0] + lax.ppermute(pieces[1], "core", [(0, 1), (1, 0)])
    both = both.reshape(2, 4, 4, 96, W)
    first = first_phase(both[0], "x")
    second = first_phase(both[1], "z")
    return jnp.stack([second_phase(first, "z"), second_phase(second, "x")])[None]


TERM = ("z", "x", "core")


def shards(left_env, right_env, mps, psi, coef, sector_sizes, pattern):
    place = jnp.stack([lax.axis_index(a) for a in ("site",) + TERM]).astype(jnp.int32)
    ints = jnp.concatenate([place, sector_sizes, pattern[0]])
    floats = coef[0, 0]
    nothing = jnp.zeros((W, W), f32)
    arrivals, environs, held = {}, {}, ()
    for step in range(LAST):
        environ = update_step(
            step, ints, floats, arrivals.get(step, nothing), arrivals.get(step - 1, nothing), left_env[0], mps[0], held)
        environs[step] = environ
        if step + LAG < LAST:
            arrivals[step + LAG] = lax.ppermute(environ, "site", [(0, 1), (1, 2), (2, 3)])
        q = step - LAG * (SITES - 1)
        if q >= 0:
            held = apply_step(
                q, ints, floats, [environs[q + LAG * k] for k in range(SITES)], psi[0], right_env[0, 0], held)
    return reduced(*held)


def solution(mesh):
    fine = Mesh(mesh.devices.reshape(4, 4, 4, 2), ("site", "z", "x", "core"))
    term = ("z", "x", "core")
    return jax.shard_map(
        shards,
        mesh=fine,
        in_specs=(
            P(term, None, None, None),
            P("site", term, None, None, None),
            P("site", None, None, None, None),
            P("site", None, None, None, None),
            P("site", term, None),
            P(),
            P(term, None),
        ),
        out_specs=P("site", None, term, None),
        check_vma=False,
    )
```

```python
import jax
import jax.numpy as jnp
from jax import lax
from jax.experimental import pallas as pl
from jax.experimental.pallas import tpu as pltpu
from jax.sharding import Mesh, PartitionSpec as P


f32, bf16 = jnp.float32, jnp.bfloat16
W = 256
NQ = 12
ROWS = 32
SITES = 4
LAG = 2


def halves(x):
    high = x.astype(bf16)
    return high, (x - high.astype(f32)).astype(bf16)


def product(a, b, dims):
    (ah, al), (bh, bl) = a, b

    def dot(u, v):
        return lax.dot_general(u, v, (dims, ((), ())), preferred_element_type=f32)

    return dot(ah, bh) + (dot(ah, bl) + dot(al, bh))


def framed(x, rows, columns):
    i = lax.broadcasted_iota(jnp.int32, x.shape, 0)
    j = lax.broadcasted_iota(jnp.int32, x.shape, 1)
    return jnp.where((i < rows) & (j < columns), x, 0.0)


LAST = NQ + LAG * (SITES - 1)
SCALAR = pl.BlockSpec(memory_space=pltpu.SMEM)
LOCAL = pl.BlockSpec(memory_space=pltpu.VMEM)
FAR = pl.BlockSpec(memory_space=pltpu.HBM)
GRANT = pltpu.CompilerParams(vmem_limit_bytes=8 * 2**20)
EARLY = 9


def update_part(q, ints, floats, arrived, previous, left, mps):
    site = ints[0]
    below = jnp.maximum(q - 1, 0)
    size, under = ints[4 + q], ints[4 + below]
    c0 = jnp.where(site == 0, ints[16 + q].astype(f32), 1.0) * floats[0]
    c1 = jnp.where(site == 0, ints[16 + below].astype(f32), 1.0) * floats[1]
    now = jnp.where(site == 0, left[q], arrived[...])
    before = jnp.where(site == 0, left[below], previous[...])
    before = jnp.where(q > 0, before, 0.0)
    s = framed(mps[0, q], size, size)
    u = framed(mps[1, below], under, size)
    first = c0 * product(halves(now), halves(s), ((1,), (0,)))
    second = c1 * product(halves(before), halves(u), ((1,), (0,)))
    return product(halves(s.T), halves(first), ((1,), (0,))) + product(
        halves(u.T), halves(second), ((1,), (0,)))


def apply_part(q, ints, floats, environs, psi, rights, pieces, results, stores):
    site, my_x, core = ints[0], ints[2], ints[3]
    e = environs[0][...]
    for k in range(1, SITES):
        e = jnp.where(site == k, environs[k][...], e)
    e = halves(e)
    scales = [floats[2] * ints[16 + q].astype(f32)]
    if q < NQ - 1:
        scales.append(floats[3] * ints[17 + q].astype(f32))
    for state in range(2):
        if q + state < NQ:
            n = ints[4 + q + state]
            part = scales[state] * product(e, halves(psi[state, q]), ((1,), (0,)))
            results[state] = product(halves(part), halves(framed(rights[q + state], n, n)), ((1,), (1,)))
        else:
            results[state] = jnp.zeros((W, W), f32)
        for i in range(W // ROWS):
            owner, third = divmod((W // ROWS) * q + i, 3)
            group = owner // 8 if q < EARLY else 0
            x = ((owner // 2) % 4 - my_x + 4) % 4
            sent = core if owner % 2 == 0 else 1 - core
            pltpu.make_async_copy(
                results.at[state, pl.ds(ROWS * i, ROWS)], pieces.at[sent, state, group, x, third], stores).start()
    pltpu.make_async_copy(results, psi.at[:, 0], stores).wait()


def update_step(step, ints, floats, arrived, previous, left, mps, held):
    def kernel(ints, floats, arrived, previous, left, mps, *rest):
        environ = rest[-1]
        q = step - LAG * ints[0]

        @pl.when((q >= 0) & (q < NQ))
        def _():
            environ[...] = update_part(q, ints, floats, arrived, previous, left, mps)

    return pl.pallas_call(
        kernel, in_specs=[SCALAR] * 2 + [LOCAL] * 4 + [FAR] * len(held), out_specs=LOCAL, out_shape=jax.ShapeDtypeStruct((W, W), f32),
        compiler_params=GRANT,
    )(ints, floats, arrived, previous, left, mps, *held)


def apply_step(q, ints, floats, environs, psi, rights, held):
    def kernel(ints, floats, *refs):
        psi, rights = refs[SITES:SITES + 2]
        apply_part(q, ints, floats, refs[:SITES], psi, rights, *refs[-3:])

    operands = (*environs, psi, rights)
    return pl.pallas_call(
        kernel,
        in_specs=[SCALAR] * 2 + [LOCAL] * len(operands) + [FAR] * len(held),
        out_specs=[FAR],
        out_shape=[jax.ShapeDtypeStruct((2, 2, 3 if q < EARLY else 1, 4, 3, ROWS, W), f32)],
        scratch_shapes=[pltpu.VMEM((2, W, W), f32), pltpu.SemaphoreType.DMA],
        input_output_aliases={2 + len(operands): 0} if q not in (0, EARLY) else {},
        compiler_params=GRANT,
    )(ints, floats, *operands, *held)


def turned(x, axis, by):
    return lax.ppermute(x, axis, [(i, (i + by) % 4) for i in range(4)])


def first_phase(both, axis):
    up = turned(both[2, :2], axis, 1)
    down = turned(both[2, 2:], axis, -1)
    ahead = jnp.concatenate([both[1, :2] + up, both[1, 2:]])
    behind = jnp.concatenate([both[3, :2], both[3, 2:] + down])
    return both[0] + turned(ahead, axis, 1) + turned(behind, axis, -1)


def second_phase(line, axis):
    even = lax.axis_index(axis) % 2 == 0
    given = jnp.stack([jnp.where(even, line[1], line[3]), line[2]])
    taken = lax.ppermute(given, axis, [(i, i ^ 1) for i in range(4)])
    rest = jnp.where(even, line[3], line[1]) + taken[1]
    return (line[0] + taken[0]) + lax.ppermute(rest, axis, [(i, i ^ 3) for i in range(4)])


def combine_kernel(ints, early, early_got, late, late_got, out):
    for group in range(4):
        z = (group - ints[1] + 4) % 4
        own, got, g = (early, early_got, group) if group < 3 else (late, late_got, 0)
        for x in range(4):
            out[0, x, z] = own[0, 0, g, x] + got[0, g, x]
            out[1, z, x] = own[0, 1, g, x] + got[1, g, x]


def swapped(pieces):
    return lax.ppermute(pieces[1], "core", [(0, 1), (1, 0)])


def reduced(ints, early, early_got, late, late_got):
    shape = (4, 96, W)
    parts = (early.reshape(2, 2, 3, *shape), early_got.reshape(2, 3, *shape),
             late.reshape(2, 2, 1, *shape), late_got.reshape(2, 1, *shape))
    both = pl.pallas_call(
        combine_kernel, in_specs=[SCALAR] + [LOCAL] * 4, out_specs=LOCAL,
        out_shape=jax.ShapeDtypeStruct((2, 4) + shape, f32), compiler_params=GRANT, name="combine",
    )(ints, *parts)
    first = first_phase(both[0], "x")
    second = first_phase(both[1], "z")
    return jnp.stack([second_phase(first, "z"), second_phase(second, "x")])[None]


TERM = ("z", "x", "core")


def shards(left_env, right_env, mps, psi, coef, sector_sizes, pattern):
    place = jnp.stack([lax.axis_index(a) for a in ("site",) + TERM]).astype(jnp.int32)
    ints = jnp.concatenate([place, sector_sizes, pattern[0]])
    floats = coef[0, 0]
    nothing = jnp.zeros((W, W), f32)
    arrivals, environs, held = {}, {}, ()
    for step in range(LAST):
        environ = update_step(
            step, ints, floats, arrivals.get(step, nothing), arrivals.get(step - 1, nothing), left_env[0], mps[0], held)
        environs[step] = environ
        if step + LAG < LAST:
            arrivals[step + LAG] = lax.ppermute(environ, "site", [(0, 1), (1, 2), (2, 3)])
        q = step - LAG * (SITES - 1)
        if q >= 0:
            if q == EARLY:
                early = held
                early_got = swapped(early[0])
            held = apply_step(
                q, ints, floats, [environs[q + LAG * k] for k in range(SITES)], psi[0], right_env[0, 0], held)
    return reduced(ints, early[0], early_got, held[0], swapped(held[0]))


def solution(mesh):
    fine = Mesh(mesh.devices.reshape(4, 4, 4, 2), ("site", "z", "x", "core"))
    term = ("z", "x", "core")
    return jax.shard_map(
        shards,
        mesh=fine,
        in_specs=(
            P(term, None, None, None),
            P("site", term, None, None, None),
            P("site", None, None, None, None),
            P("site", None, None, None, None),
            P("site", term, None),
            P(),
            P(term, None),
        ),
        out_specs=P("site", None, term, None),
        check_vma=False,
    )
```

```python
import jax
import jax.numpy as jnp
from jax import lax
from jax.experimental import pallas as pl
from jax.experimental.pallas import tpu as pltpu
from jax.sharding import Mesh, PartitionSpec as P


f32, bf16 = jnp.float32, jnp.bfloat16
W = 256
NQ = 12
ROWS = 32
SITES = 4
LAG = 2


def halves(x):
    high = x.astype(bf16)
    return high, (x - high.astype(f32)).astype(bf16)


def product(a, b, dims):
    (ah, al), (bh, bl) = a, b

    def dot(u, v):
        return lax.dot_general(u, v, (dims, ((), ())), preferred_element_type=f32)

    return dot(ah, bh) + (dot(ah, bl) + dot(al, bh))


def framed(x, rows, columns):
    i = lax.broadcasted_iota(jnp.int32, x.shape, 0)
    j = lax.broadcasted_iota(jnp.int32, x.shape, 1)
    return jnp.where((i < rows) & (j < columns), x, 0.0)


LAST = NQ + LAG * (SITES - 1)
SCALAR = pl.BlockSpec(memory_space=pltpu.SMEM)
LOCAL = pl.BlockSpec(memory_space=pltpu.VMEM)
FAR = pl.BlockSpec(memory_space=pltpu.HBM)
GRANT = pltpu.CompilerParams(vmem_limit_bytes=8 * 2**20)
BUFFER = jax.ShapeDtypeStruct((2, 2, 4, 4, 3, ROWS, W), f32)


def update_part(q, ints, floats, arrived, previous, left, mps):
    site = ints[0]
    below = jnp.maximum(q - 1, 0)
    size, under = ints[4 + q], ints[4 + below]
    c0 = jnp.where(site == 0, ints[16 + q].astype(f32), 1.0) * floats[0]
    c1 = jnp.where(site == 0, ints[16 + below].astype(f32), 1.0) * floats[1]
    now = jnp.where(site == 0, left[q], arrived[...])
    before = jnp.where(site == 0, left[below], previous[...])
    before = jnp.where(q > 0, before, 0.0)
    s = framed(mps[0, q], size, size)
    u = framed(mps[1, below], under, size)
    first = c0 * product(halves(now), halves(s), ((1,), (0,)))
    second = c1 * product(halves(before), halves(u), ((1,), (0,)))
    return product(halves(s.T), halves(first), ((1,), (0,))) + product(
        halves(u.T), halves(second), ((1,), (0,)))


def apply_part(q, ints, floats, environs, psi, rights, pieces, results, stores):
    site, my_z, my_x, core = ints[0], ints[1], ints[2], ints[3]
    e = environs[0][...]
    for k in range(1, SITES):
        e = jnp.where(site == k, environs[k][...], e)
    e = halves(e)
    scales = [floats[2] * ints[16 + q].astype(f32)]
    if q < NQ - 1:
        scales.append(floats[3] * ints[17 + q].astype(f32))
    for state in range(2):
        if q + state < NQ:
            n = ints[4 + q + state]
            part = scales[state] * product(e, halves(psi[state, q]), ((1,), (0,)))
            results[state] = product(halves(part), halves(framed(rights[q + state], n, n)), ((1,), (1,)))
        else:
            results[state] = jnp.zeros((W, W), f32)
        for i in range(W // ROWS):
            owner, third = divmod((W // ROWS) * q + i, 3)
            z = (owner // 8 - my_z + 4) % 4
            x = ((owner // 2) % 4 - my_x + 4) % 4
            sent = core if owner % 2 == 0 else 1 - core
            near, far = ((x, z), (z, x))[state]
            pltpu.make_async_copy(
                results.at[state, pl.ds(ROWS * i, ROWS)], pieces.at[sent, state, near, far, third], stores).start()
    pltpu.make_async_copy(results, psi.at[:, 0], stores).wait()


def early_step(q, ints, floats, left, mps):
    def kernel(ints, floats, left, mps, environ, blocks, sems):
        @pl.when(ints[0] == 0)
        def _():
            sources = [left.at[q], mps.at[0, q]] + ([left.at[q - 1], mps.at[1, q - 1]] if q else [])
            copies = [pltpu.make_async_copy(source, blocks.at[i], sems.at[i]) for i, source in enumerate(sources)]
            for copy in copies:
                copy.start()
            for copy in copies:
                copy.wait()
            size = ints[4 + q]
            s = framed(blocks[1], size, size)
            first = floats[0] * ints[16 + q].astype(f32) * product(halves(blocks[0]), halves(s), ((1,), (0,)))
            moved = product(halves(s.T), halves(first), ((1,), (0,)))
            if q:
                u = framed(blocks[3], ints[3 + q], size)
                second = floats[1] * ints[15 + q].astype(f32) * product(halves(blocks[2]), halves(u), ((1,), (0,)))
                moved = moved + product(halves(u.T), halves(second), ((1,), (0,)))
            environ[...] = moved

    return pl.pallas_call(
        kernel, in_specs=[SCALAR] * 2 + [FAR] * 2, out_specs=LOCAL, out_shape=jax.ShapeDtypeStruct((W, W), f32),
        scratch_shapes=[pltpu.VMEM((4, W, W), f32), pltpu.SemaphoreType.DMA((4,))],
        compiler_params=pltpu.CompilerParams(vmem_limit_bytes=52 * 2**20),
    )(ints, floats, left, mps)


def update_step(step, ints, floats, arrived, previous, left, mps, held):
    def kernel(ints, floats, arrived, previous, left, mps, *rest):
        environ = rest[-1]
        q = step - LAG * ints[0]

        @pl.when((q >= 0) & (q < NQ))
        def _():
            environ[...] = update_part(q, ints, floats, arrived, previous, left, mps)

    return pl.pallas_call(
        kernel, in_specs=[SCALAR] * 2 + [LOCAL] * 4 + [FAR] * len(held), out_specs=LOCAL, out_shape=jax.ShapeDtypeStruct((W, W), f32),
        compiler_params=GRANT,
    )(ints, floats, arrived, previous, left, mps, *held)


def apply_step(q, ints, floats, environs, psi, rights, held):
    def kernel(ints, floats, *refs):
        psi, rights = refs[SITES:SITES + 2]
        apply_part(q, ints, floats, refs[:SITES], psi, rights, *refs[-3:])

    operands = (*environs, psi, rights)
    return pl.pallas_call(
        kernel,
        in_specs=[SCALAR] * 2 + [LOCAL] * len(operands) + [FAR] * len(held),
        out_specs=[FAR],
        out_shape=[BUFFER],
        scratch_shapes=[pltpu.VMEM((2, W, W), f32), pltpu.SemaphoreType.DMA],
        input_output_aliases={2 + len(operands): 0} if held else {},
        compiler_params=GRANT,
    )(ints, floats, *operands, *held)


def turned(x, axis, by):
    return lax.ppermute(x, axis, [(i, (i + by) % 4) for i in range(4)])


def first_phase(both, axis):
    up = turned(both[2, :2], axis, 1)
    down = turned(both[2, 2:], axis, -1)
    ahead = jnp.concatenate([both[1, :2] + up, both[1, 2:]])
    behind = jnp.concatenate([both[3, :2], both[3, 2:] + down])
    return both[0] + turned(ahead, axis, 1) + turned(behind, axis, -1)


def second_phase(line, axis):
    return (line[0] + turned(line[1], axis, 1)) + (turned(line[3], axis, -1) + turned(line[2], axis, 2))


def reduced(pieces):
    both = pieces[0] + lax.ppermute(pieces[1], "core", [(0, 1), (1, 0)])
    both = both.reshape(2, 4, 4, 96, W)
    first = first_phase(both[0], "x")
    second = first_phase(both[1], "z")
    return jnp.stack([second_phase(first, "z"), second_phase(second, "x")])[None]


TERM = ("z", "x", "core")


def shards(left_env, right_env, mps, psi, coef, sector_sizes, pattern):
    place = jnp.stack([lax.axis_index(a) for a in ("site",) + TERM]).astype(jnp.int32)
    ints = jnp.concatenate([place, sector_sizes, pattern[0]])
    floats = coef[0, 0]
    nothing = jnp.zeros((W, W), f32)
    arrivals, environs, held = {}, {}, ()
    for step in range(LAST):
        if step < LAG:
            environ = early_step(step, ints, floats, left_env[0], mps[0])
        else:
            environ = update_step(
                step, ints, floats, arrivals[step], arrivals.get(step - 1, nothing), left_env[0], mps[0], held)
        environs[step] = environ
        if step + LAG < LAST:
            arrivals[step + LAG] = lax.ppermute(environ, "site", [(0, 1), (1, 2), (2, 3)])
        q = step - LAG * (SITES - 1)
        if q >= 0:
            held = apply_step(
                q, ints, floats, [environs[q + LAG * k] for k in range(SITES)], psi[0], right_env[0, 0], held)
    return reduced(*held)


def solution(mesh):
    fine = Mesh(mesh.devices.reshape(4, 4, 4, 2), ("site", "z", "x", "core"))
    term = ("z", "x", "core")
    return jax.shard_map(
        shards,
        mesh=fine,
        in_specs=(
            P(term, None, None, None),
            P("site", term, None, None, None),
            P("site", None, None, None, None),
            P("site", None, None, None, None),
            P("site", term, None),
            P(),
            P(term, None),
        ),
        out_specs=P("site", None, term, None),
        check_vma=False,
    )
```

```python
import jax
import jax.numpy as jnp
from jax import lax
from jax.experimental import pallas as pl
from jax.experimental.pallas import tpu as pltpu
from jax.sharding import Mesh, PartitionSpec as P


f32, bf16 = jnp.float32, jnp.bfloat16
W = 256
NQ = 12
ROWS = 32
SITES = 4
LAG = 2


def halves(x):
    high = x.astype(bf16)
    return high, (x - high.astype(f32)).astype(bf16)


def product(a, b, dims):
    (ah, al), (bh, bl) = a, b

    def dot(u, v):
        return lax.dot_general(u, v, (dims, ((), ())), preferred_element_type=f32)

    return dot(ah, bh) + (dot(ah, bl) + dot(al, bh))


def framed(x, rows, columns):
    i = lax.broadcasted_iota(jnp.int32, x.shape, 0)
    j = lax.broadcasted_iota(jnp.int32, x.shape, 1)
    return jnp.where((i < rows) & (j < columns), x, 0.0)


LAST = NQ + LAG * (SITES - 1)
SCALAR = pl.BlockSpec(memory_space=pltpu.SMEM)
LOCAL = pl.BlockSpec(memory_space=pltpu.VMEM)
FAR = pl.BlockSpec(memory_space=pltpu.HBM)
GRANT = pltpu.CompilerParams(vmem_limit_bytes=8 * 2**20)
BUFFER = jax.ShapeDtypeStruct((2, 4, 4, 3, ROWS, W), f32)


def update_part(q, ints, floats, arrived, previous, left, mps):
    site = ints[0]
    below = jnp.maximum(q - 1, 0)
    size, under = ints[4 + q], ints[4 + below]
    c0 = jnp.where(site == 0, ints[16 + q].astype(f32), 1.0) * floats[0]
    c1 = jnp.where(site == 0, ints[16 + below].astype(f32), 1.0) * floats[1]
    now = jnp.where(site == 0, left[q], arrived[...])
    before = jnp.where(site == 0, left[below], previous[...])
    before = jnp.where(q > 0, before, 0.0)
    s = framed(mps[0, q], size, size)
    u = framed(mps[1, below], under, size)
    first = c0 * product(halves(now), halves(s), ((1,), (0,)))
    second = c1 * product(halves(before), halves(u), ((1,), (0,)))
    return product(halves(s.T), halves(first), ((1,), (0,))) + product(
        halves(u.T), halves(second), ((1,), (0,)))


def apply_part(q, ints, floats, environs, psi, rights, pieces, results, stores):
    site, my_z, my_x, core = ints[0], ints[1], ints[2], ints[3]
    e = environs[0][...]
    for k in range(1, SITES):
        e = jnp.where(site == k, environs[k][...], e)
    e = halves(e)
    work = [(0, q)] + [(1, q)] * (q < NQ - 1) + [(1, NQ - 1)] * (q == NQ - 2)
    for slot, (state, at) in enumerate(work):
        if at + state < NQ:
            n = ints[4 + q + state]
            c = floats[2 + state] * ints[16 + q + state].astype(f32)
            part = c * product(e, halves(psi[state, q]), ((1,), (0,)))
            results[slot] = product(halves(part), halves(framed(rights[q + state], n, n)), ((1,), (1,)))
        else:
            results[slot] = jnp.zeros((W, W), f32)
        for i in range(W // ROWS):
            owner, third = divmod((W // ROWS) * at + i, 3)
            z = (owner // 8 - my_z + 4) % 4
            x = ((owner // 2) % 4 - my_x + 4) % 4
            sent = core if owner % 2 == 0 else 1 - core
            near, far = ((x, z), (z, x))[state]
            pltpu.make_async_copy(
                results.at[slot, pl.ds(ROWS * i, ROWS)], pieces[state].at[sent, near, far, third], stores).start()
    stored = results.at[pl.ds(0, len(work))]
    pltpu.make_async_copy(stored, stored, stores).wait()


def early_step(q, ints, floats, left, mps):
    def kernel(ints, floats, left, mps, environ, blocks, sems):
        @pl.when(ints[0] == 0)
        def _():
            sources = [left.at[q], mps.at[0, q]] + ([left.at[q - 1], mps.at[1, q - 1]] if q else [])
            copies = [pltpu.make_async_copy(source, blocks.at[i], sems.at[i]) for i, source in enumerate(sources)]
            for copy in copies:
                copy.start()
            for copy in copies:
                copy.wait()
            size = ints[4 + q]
            s = framed(blocks[1], size, size)
            first = floats[0] * ints[16 + q].astype(f32) * product(halves(blocks[0]), halves(s), ((1,), (0,)))
            moved = product(halves(s.T), halves(first), ((1,), (0,)))
            if q:
                u = framed(blocks[3], ints[3 + q], size)
                second = floats[1] * ints[15 + q].astype(f32) * product(halves(blocks[2]), halves(u), ((1,), (0,)))
                moved = moved + product(halves(u.T), halves(second), ((1,), (0,)))
            environ[...] = moved

    return pl.pallas_call(
        kernel, in_specs=[SCALAR] * 2 + [FAR] * 2, out_specs=LOCAL, out_shape=jax.ShapeDtypeStruct((W, W), f32),
        scratch_shapes=[pltpu.VMEM((4, W, W), f32), pltpu.SemaphoreType.DMA((4,))],
        compiler_params=pltpu.CompilerParams(vmem_limit_bytes=52 * 2**20),
    )(ints, floats, left, mps)


def update_step(step, ints, floats, arrived, previous, left, mps, held):
    def kernel(ints, floats, arrived, previous, left, mps, *rest):
        environ = rest[-1]
        q = step - LAG * ints[0]

        @pl.when((q >= 0) & (q < NQ))
        def _():
            environ[...] = update_part(q, ints, floats, arrived, previous, left, mps)

    return pl.pallas_call(
        kernel, in_specs=[SCALAR] * 2 + [LOCAL] * 4 + [FAR] * len(held), out_specs=LOCAL, out_shape=jax.ShapeDtypeStruct((W, W), f32),
        compiler_params=GRANT,
    )(ints, floats, arrived, previous, left, mps, *held)


def apply_step(q, ints, floats, environs, psi, rights, held):
    operands = (*environs, psi, rights)
    states = 1 if q == NQ - 1 else 2

    def kernel(ints, floats, *refs):
        psi, rights = refs[SITES:SITES + 2]
        apply_part(q, ints, floats, refs[:SITES], psi, rights, refs[-2 - states:-2], *refs[-2:])

    return pl.pallas_call(
        kernel,
        in_specs=[SCALAR] * 2 + [LOCAL] * len(operands) + [FAR] * len(held),
        out_specs=[FAR] * states,
        out_shape=[BUFFER] * states,
        scratch_shapes=[pltpu.VMEM((3, W, W), f32), pltpu.SemaphoreType.DMA],
        input_output_aliases={2 + len(operands) + i: i for i in range(len(held))},
        compiler_params=GRANT,
    )(ints, floats, *operands, *held)


def turned(x, axis, by):
    return lax.ppermute(x, axis, [(i, (i + by) % 4) for i in range(4)])


def first_phase(both, axis):
    up = turned(both[2, :2], axis, 1)
    down = turned(both[2, 2:], axis, -1)
    ahead = jnp.concatenate([both[1, :2] + up, both[1, 2:]])
    behind = jnp.concatenate([both[3, :2], both[3, 2:] + down])
    return both[0] + turned(ahead, axis, 1) + turned(behind, axis, -1)


def second_phase(line, axis):
    return (line[0] + turned(line[1], axis, 1)) + (turned(line[3], axis, -1) + turned(line[2], axis, 2))


def swapped(pieces):
    return lax.ppermute(pieces[1], "core", [(0, 1), (1, 0)])


def reduced(first, first_got, second, second_got):
    shape = (4, 4, 96, W)
    second = (second[0] + second_got).reshape(shape)
    second, first_got = lax.optimization_barrier((second, first_got))
    first = (first[0] + first_got).reshape(shape)
    second = first_phase(second, "z")
    first = first_phase(first, "x")
    return jnp.stack([second_phase(first, "z"), second_phase(second, "x")])[None]


TERM = ("z", "x", "core")


def shards(left_env, right_env, mps, psi, coef, sector_sizes, pattern):
    place = jnp.stack([lax.axis_index(a) for a in ("site",) + TERM]).astype(jnp.int32)
    ints = jnp.concatenate([place, sector_sizes, pattern[0]])
    floats = coef[0, 0]
    nothing = jnp.zeros((W, W), f32)
    arrivals, environs, held = {}, {}, ()
    for step in range(LAST):
        if step < LAG:
            environ = early_step(step, ints, floats, left_env[0], mps[0])
        else:
            environ = update_step(
                step, ints, floats, arrivals[step], arrivals.get(step - 1, nothing), left_env[0], mps[0], held)
        environs[step] = environ
        if step + LAG < LAST:
            arrivals[step + LAG] = lax.ppermute(environ, "site", [(0, 1), (1, 2), (2, 3)])
        q = step - LAG * (SITES - 1)
        if q == NQ - 1:
            second, held = held[1], held[:1]
            second_got = swapped(second)
        if q >= 0:
            held = apply_step(
                q, ints, floats, [environs[q + LAG * k] for k in range(SITES)], psi[0], right_env[0, 0], held)
    return reduced(held[0], swapped(held[0]), second, second_got)


def solution(mesh):
    fine = Mesh(mesh.devices.reshape(4, 4, 4, 2), ("site", "z", "x", "core"))
    term = ("z", "x", "core")
    return jax.shard_map(
        shards,
        mesh=fine,
        in_specs=(
            P(term, None, None, None),
            P("site", term, None, None, None),
            P("site", None, None, None, None),
            P("site", None, None, None, None),
            P("site", term, None),
            P(),
            P(term, None),
        ),
        out_specs=P("site", None, term, None),
        check_vma=False,
    )
```

```python
import jax
import jax.numpy as jnp
from jax import lax
from jax.experimental import pallas as pl
from jax.experimental.pallas import tpu as pltpu
from jax.sharding import Mesh, PartitionSpec as P


f32, bf16 = jnp.float32, jnp.bfloat16
W = 256
NQ = 12
ROWS = 32
SITES = 4
LAG = 2


def halves(x):
    high = x.astype(bf16)
    return high, (x - high.astype(f32)).astype(bf16)


def product(a, b, dims):
    (ah, al), (bh, bl) = a, b

    def dot(u, v):
        return lax.dot_general(u, v, (dims, ((), ())), preferred_element_type=f32)

    return dot(ah, bh) + (dot(ah, bl) + dot(al, bh))


def framed(x, rows, columns):
    i = lax.broadcasted_iota(jnp.int32, x.shape, 0)
    j = lax.broadcasted_iota(jnp.int32, x.shape, 1)
    return jnp.where((i < rows) & (j < columns), x, 0.0)


LAST = NQ + LAG * (SITES - 1)
SCALAR = pl.BlockSpec(memory_space=pltpu.SMEM)
LOCAL = pl.BlockSpec(memory_space=pltpu.VMEM)
FAR = pl.BlockSpec(memory_space=pltpu.HBM)
GRANT = pltpu.CompilerParams(vmem_limit_bytes=8 * 2**20)
BUFFER = jax.ShapeDtypeStruct((2, 4, 4, 3, ROWS, W), f32)


def update_part(q, ints, floats, arrived, previous, left, mps):
    site = ints[0]
    below = jnp.maximum(q - 1, 0)
    size, under = ints[4 + q], ints[4 + below]
    c0 = jnp.where(site == 0, ints[16 + q].astype(f32), 1.0) * floats[0]
    c1 = jnp.where(site == 0, ints[16 + below].astype(f32), 1.0) * floats[1]
    now = jnp.where(site == 0, left[q], arrived[...])
    before = jnp.where(site == 0, left[below], previous[...])
    before = jnp.where(q > 0, before, 0.0)
    s = framed(mps[0, q], size, size)
    u = framed(mps[1, below], under, size)
    first = c0 * product(halves(now), halves(s), ((1,), (0,)))
    second = c1 * product(halves(before), halves(u), ((1,), (0,)))
    return product(halves(s.T), halves(first), ((1,), (0,))) + product(
        halves(u.T), halves(second), ((1,), (0,)))


def apply_part(q, ints, floats, environs, psi, rights, pieces, results, stores):
    site, my_z, my_x, core = ints[0], ints[1], ints[2], ints[3]
    e = environs[0][...]
    for k in range(1, SITES):
        e = jnp.where(site == k, environs[k][...], e)
    e = halves(e)
    work = [(0, q)] + [(1, q)] * (q < NQ - 1) + [(1, NQ - 1)] * (q == NQ - 2)
    for slot, (state, at) in enumerate(work):
        if at + state < NQ:
            n = ints[4 + q + state]
            c = floats[2 + state] * ints[16 + q + state].astype(f32)
            part = c * product(e, halves(psi[state, q]), ((1,), (0,)))
            results[slot] = product(halves(part), halves(framed(rights[q + state], n, n)), ((1,), (1,)))
        else:
            results[slot] = jnp.zeros((W, W), f32)
        for i in range(W // ROWS):
            owner, third = divmod((W // ROWS) * at + i, 3)
            z = (owner // 8 - my_z + 4) % 4
            x = ((owner // 2) % 4 - my_x + 4) % 4
            sent = core if owner % 2 == 0 else 1 - core
            near, far = ((x, z), (z, x))[state]
            pltpu.make_async_copy(
                results.at[slot, pl.ds(ROWS * i, ROWS)], pieces[state].at[sent, near, far, third], stores).start()
    stored = results.at[pl.ds(0, len(work))]
    pltpu.make_async_copy(stored, stored, stores).wait()


def early_step(q, ints, floats, left, mps):
    def kernel(ints, floats, left, mps, environ, blocks, sems):
        @pl.when(ints[0] == 0)
        def _():
            sources = [left.at[q], mps.at[0, q]] + ([left.at[q - 1], mps.at[1, q - 1]] if q else [])
            copies = [pltpu.make_async_copy(source, blocks.at[i], sems.at[i]) for i, source in enumerate(sources)]
            for copy in copies:
                copy.start()
            for copy in copies:
                copy.wait()
            size = ints[4 + q]
            s = framed(blocks[1], size, size)
            first = floats[0] * ints[16 + q].astype(f32) * product(halves(blocks[0]), halves(s), ((1,), (0,)))
            moved = product(halves(s.T), halves(first), ((1,), (0,)))
            if q:
                u = framed(blocks[3], ints[3 + q], size)
                second = floats[1] * ints[15 + q].astype(f32) * product(halves(blocks[2]), halves(u), ((1,), (0,)))
                moved = moved + product(halves(u.T), halves(second), ((1,), (0,)))
            environ[...] = moved

    return pl.pallas_call(
        kernel, in_specs=[SCALAR] * 2 + [FAR] * 2, out_specs=LOCAL, out_shape=jax.ShapeDtypeStruct((W, W), f32),
        scratch_shapes=[pltpu.VMEM((4, W, W), f32), pltpu.SemaphoreType.DMA((4,))],
        compiler_params=pltpu.CompilerParams(vmem_limit_bytes=52 * 2**20),
    )(ints, floats, left, mps)


def update_step(step, ints, floats, arrived, previous, left, mps, held):
    def kernel(ints, floats, arrived, previous, left, mps, *rest):
        environ = rest[-1]
        q = step - LAG * ints[0]

        @pl.when((q >= 0) & (q < NQ))
        def _():
            environ[...] = update_part(q, ints, floats, arrived, previous, left, mps)

    return pl.pallas_call(
        kernel, in_specs=[SCALAR] * 2 + [LOCAL] * 4 + [FAR] * len(held), out_specs=LOCAL, out_shape=jax.ShapeDtypeStruct((W, W), f32),
        compiler_params=GRANT,
    )(ints, floats, arrived, previous, left, mps, *held)


def apply_step(q, ints, floats, environs, psi, rights, held):
    operands = (*environs, psi, rights)
    states = 1 if q == NQ - 1 else 2

    def kernel(ints, floats, *refs):
        psi, rights = refs[SITES:SITES + 2]
        apply_part(q, ints, floats, refs[:SITES], psi, rights, refs[-2 - states:-2], *refs[-2:])

    return pl.pallas_call(
        kernel,
        in_specs=[SCALAR] * 2 + [LOCAL] * len(operands) + [FAR] * len(held),
        out_specs=[FAR] * states,
        out_shape=[BUFFER] * states,
        scratch_shapes=[pltpu.VMEM((3, W, W), f32), pltpu.SemaphoreType.DMA],
        input_output_aliases={2 + len(operands) + i: i for i in range(len(held))},
        compiler_params=GRANT,
    )(ints, floats, *operands, *held)


def turned(x, axis, by):
    return lax.ppermute(x, axis, [(i, (i + by) % 4) for i in range(4)])


def first_phase(far, own, ahead, behind, axis):
    up = turned(far[0], axis, 1)
    down = turned(far[1], axis, -1)
    ahead = jnp.concatenate([ahead[:2] + up, ahead[2:]])
    behind = jnp.concatenate([behind[:2], behind[2:] + down])
    return own + turned(ahead, axis, 1) + turned(behind, axis, -1)


def second_phase(line, axis):
    return (line[0] + turned(line[1], axis, 1)) + (turned(line[3], axis, -1) + turned(line[2], axis, 2))


def swapped(pieces):
    return lax.ppermute(pieces[1], "core", [(0, 1), (1, 0)])


def reduced(first, first_got, second, second_got):
    shape = (4, 4, 96, W)
    kept, got = second[0].reshape(shape), second_got.reshape(shape)
    far = kept[2, :2] + got[2, :2], kept[2, 2:] + got[2, 2:]
    rest = [kept[i] + got[i] for i in (0, 1, 3)]
    *rest, first_got = lax.optimization_barrier((*rest, first_got))
    second = first_phase(far, *rest, "z")
    first = (first[0] + first_got).reshape(shape)
    first = first_phase((first[2, :2], first[2, 2:]), first[0], first[1], first[3], "x")
    return jnp.stack([second_phase(first, "z"), second_phase(second, "x")])[None]


TERM = ("z", "x", "core")


def shards(left_env, right_env, mps, psi, coef, sector_sizes, pattern):
    place = jnp.stack([lax.axis_index(a) for a in ("site",) + TERM]).astype(jnp.int32)
    ints = jnp.concatenate([place, sector_sizes, pattern[0]])
    floats = coef[0, 0]
    nothing = jnp.zeros((W, W), f32)
    arrivals, environs, held = {}, {}, ()
    for step in range(LAST):
        if step < LAG:
            environ = early_step(step, ints, floats, left_env[0], mps[0])
        else:
            environ = update_step(
                step, ints, floats, arrivals[step], arrivals.get(step - 1, nothing), left_env[0], mps[0], held)
        environs[step] = environ
        if step + LAG < LAST:
            arrivals[step + LAG] = lax.ppermute(environ, "site", [(0, 1), (1, 2), (2, 3)])
        q = step - LAG * (SITES - 1)
        if q == NQ - 1:
            second, held = held[1], held[:1]
            second_got = swapped(second)
        if q >= 0:
            held = apply_step(
                q, ints, floats, [environs[q + LAG * k] for k in range(SITES)], psi[0], right_env[0, 0], held)
    first_got = swapped(held[0])
    return reduced(held[0], first_got, second, second_got)


def solution(mesh):
    fine = Mesh(mesh.devices.reshape(4, 4, 4, 2), ("site", "z", "x", "core"))
    term = ("z", "x", "core")
    return jax.shard_map(
        shards,
        mesh=fine,
        in_specs=(
            P(term, None, None, None),
            P("site", term, None, None, None),
            P("site", None, None, None, None),
            P("site", None, None, None, None),
            P("site", term, None),
            P(),
            P(term, None),
        ),
        out_specs=P("site", None, term, None),
        check_vma=False,
    )
```

```python
import jax
import jax.numpy as jnp
from jax import lax
from jax.experimental import pallas as pl
from jax.experimental.pallas import tpu as pltpu
from jax.sharding import Mesh, PartitionSpec as P


f32, bf16 = jnp.float32, jnp.bfloat16
W = 256
NQ = 12
ROWS = 32
SITES = 4
LAG = 2


def halves(x):
    high = x.astype(bf16)
    return high, (x - high.astype(f32)).astype(bf16)


def product(a, b, dims):
    (ah, al), (bh, bl) = a, b

    def dot(u, v):
        return lax.dot_general(u, v, (dims, ((), ())), preferred_element_type=f32)

    return dot(ah, bh) + (dot(ah, bl) + dot(al, bh))


def framed(x, rows, columns):
    i = lax.broadcasted_iota(jnp.int32, x.shape, 0)
    j = lax.broadcasted_iota(jnp.int32, x.shape, 1)
    return jnp.where((i < rows) & (j < columns), x, 0.0)


LAST = NQ + LAG * (SITES - 1)
SCALAR = pl.BlockSpec(memory_space=pltpu.SMEM)
LOCAL = pl.BlockSpec(memory_space=pltpu.VMEM)
FAR = pl.BlockSpec(memory_space=pltpu.HBM)
GRANT = pltpu.CompilerParams(vmem_limit_bytes=8 * 2**20)
BUFFER = jax.ShapeDtypeStruct((2, 4, 4, 3, ROWS, W), f32)


def update_part(q, ints, floats, arrived, previous, left, mps):
    site = ints[0]
    below = jnp.maximum(q - 1, 0)
    size, under = ints[4 + q], ints[4 + below]
    c0 = jnp.where(site == 0, ints[16 + q].astype(f32), 1.0) * floats[0]
    c1 = jnp.where(site == 0, ints[16 + below].astype(f32), 1.0) * floats[1]
    now = jnp.where(site == 0, left[q], arrived[...])
    before = jnp.where(site == 0, left[below], previous[...])
    before = jnp.where(q > 0, before, 0.0)
    s = framed(mps[0, q], size, size)
    u = framed(mps[1, below], under, size)
    first = c0 * product(halves(now), halves(s), ((1,), (0,)))
    second = c1 * product(halves(before), halves(u), ((1,), (0,)))
    return product(halves(s.T), halves(first), ((1,), (0,))) + product(
        halves(u.T), halves(second), ((1,), (0,)))


def apply_part(q, ints, floats, environs, psi, rights, pieces, results, stores):
    site, my_z, my_x, core = ints[0], ints[1], ints[2], ints[3]
    e = environs[0][...]
    for k in range(1, SITES):
        e = jnp.where(site == k, environs[k][...], e)
    e = halves(e)
    work = [(0, q)] + [(1, q)] * (q < NQ - 1) + [(1, NQ - 1)] * (q == NQ - 2)
    parts = {}
    for state, at in work:
        if at + state < NQ:
            c = floats[2 + state] * ints[16 + q + state].astype(f32)
            parts[state] = halves(c * product(e, halves(psi[state, q]), ((1,), (0,))))
    for slot, (state, at) in enumerate(work):
        if at + state < NQ:
            n = ints[4 + q + state]
            results[slot] = product(parts[state], halves(framed(rights[q + state], n, n)), ((1,), (1,)))
        else:
            results[slot] = jnp.zeros((W, W), f32)
        for i in range(W // ROWS):
            owner, third = divmod((W // ROWS) * at + i, 3)
            z = (owner // 8 - my_z + 4) % 4
            x = ((owner // 2) % 4 - my_x + 4) % 4
            sent = core if owner % 2 == 0 else 1 - core
            near, far = ((x, z), (z, x))[state]
            pltpu.make_async_copy(
                results.at[slot, pl.ds(ROWS * i, ROWS)], pieces[state].at[sent, near, far, third], stores).start()
    stored = results.at[pl.ds(0, len(work))]
    pltpu.make_async_copy(stored, stored, stores).wait()


def early_step(q, ints, floats, left, mps):
    def kernel(ints, floats, left, mps, environ, blocks, sems):
        @pl.when(ints[0] == 0)
        def _():
            sources = [left.at[q], mps.at[0, q]] + ([left.at[q - 1], mps.at[1, q - 1]] if q else [])
            copies = [pltpu.make_async_copy(source, blocks.at[i], sems.at[i]) for i, source in enumerate(sources)]
            for copy in copies:
                copy.start()
            for copy in copies:
                copy.wait()
            size = ints[4 + q]
            s = framed(blocks[1], size, size)
            first = floats[0] * ints[16 + q].astype(f32) * product(halves(blocks[0]), halves(s), ((1,), (0,)))
            moved = product(halves(s.T), halves(first), ((1,), (0,)))
            if q:
                u = framed(blocks[3], ints[3 + q], size)
                second = floats[1] * ints[15 + q].astype(f32) * product(halves(blocks[2]), halves(u), ((1,), (0,)))
                moved = moved + product(halves(u.T), halves(second), ((1,), (0,)))
            environ[...] = moved

    return pl.pallas_call(
        kernel, in_specs=[SCALAR] * 2 + [FAR] * 2, out_specs=LOCAL, out_shape=jax.ShapeDtypeStruct((W, W), f32),
        scratch_shapes=[pltpu.VMEM((4, W, W), f32), pltpu.SemaphoreType.DMA((4,))],
        compiler_params=pltpu.CompilerParams(vmem_limit_bytes=52 * 2**20),
    )(ints, floats, left, mps)


def update_step(step, ints, floats, arrived, previous, left, mps, held):
    def kernel(ints, floats, arrived, previous, left, mps, *rest):
        environ = rest[-1]
        q = step - LAG * ints[0]

        @pl.when((q >= 0) & (q < NQ))
        def _():
            environ[...] = update_part(q, ints, floats, arrived, previous, left, mps)

    return pl.pallas_call(
        kernel, in_specs=[SCALAR] * 2 + [LOCAL] * 4 + [FAR] * len(held), out_specs=LOCAL, out_shape=jax.ShapeDtypeStruct((W, W), f32),
        compiler_params=GRANT,
    )(ints, floats, arrived, previous, left, mps, *held)


def apply_step(q, ints, floats, environs, psi, rights, held):
    operands = (*environs, psi, rights)
    states = 1 if q == NQ - 1 else 2

    def kernel(ints, floats, *refs):
        psi, rights = refs[SITES:SITES + 2]
        apply_part(q, ints, floats, refs[:SITES], psi, rights, refs[-2 - states:-2], *refs[-2:])

    return pl.pallas_call(
        kernel,
        in_specs=[SCALAR] * 2 + [LOCAL] * len(operands) + [FAR] * len(held),
        out_specs=[FAR] * states,
        out_shape=[BUFFER] * states,
        scratch_shapes=[pltpu.VMEM((3, W, W), f32), pltpu.SemaphoreType.DMA],
        input_output_aliases={2 + len(operands) + i: i for i in range(len(held))},
        compiler_params=GRANT,
    )(ints, floats, *operands, *held)


def turned(x, axis, by):
    return lax.ppermute(x, axis, [(i, (i + by) % 4) for i in range(4)])


def first_phase(far, own, ahead, behind, axis):
    up = turned(far[0], axis, 1)
    down = turned(far[1], axis, -1)
    ahead = jnp.concatenate([ahead[:2] + up, ahead[2:]])
    behind = jnp.concatenate([behind[:2], behind[2:] + down])
    return own + turned(ahead, axis, 1) + turned(behind, axis, -1)


def second_phase(line, axis):
    return (line[0] + turned(line[1], axis, 1)) + (turned(line[3], axis, -1) + turned(line[2], axis, 2))


def swapped(pieces):
    return lax.ppermute(pieces[1], "core", [(0, 1), (1, 0)])


def reduced(first, first_got, second, second_got):
    shape = (4, 4, 96, W)
    kept, got = second[0].reshape(shape), second_got.reshape(shape)
    far = kept[2, :2] + got[2, :2], kept[2, 2:] + got[2, 2:]
    rest = [kept[i] + got[i] for i in (0, 1, 3)]
    *rest, first_got = lax.optimization_barrier((*rest, first_got))
    second = first_phase(far, *rest, "z")
    first = (first[0] + first_got).reshape(shape)
    first = first_phase((first[2, :2], first[2, 2:]), first[0], first[1], first[3], "x")
    return jnp.stack([second_phase(first, "z"), second_phase(second, "x")])[None]


TERM = ("z", "x", "core")


def shards(left_env, right_env, mps, psi, coef, sector_sizes, pattern):
    place = jnp.stack([lax.axis_index(a) for a in ("site",) + TERM]).astype(jnp.int32)
    ints = jnp.concatenate([place, sector_sizes, pattern[0]])
    floats = coef[0, 0]
    nothing = jnp.zeros((W, W), f32)
    arrivals, environs, held = {}, {}, ()
    for step in range(LAST):
        if step < LAG:
            environ = early_step(step, ints, floats, left_env[0], mps[0])
        else:
            environ = update_step(
                step, ints, floats, arrivals[step], arrivals.get(step - 1, nothing), left_env[0], mps[0], held)
        environs[step] = environ
        if step + LAG < LAST:
            arrivals[step + LAG] = lax.ppermute(environ, "site", [(0, 1), (1, 2), (2, 3)])
        q = step - LAG * (SITES - 1)
        if q == NQ - 1:
            second, held = held[1], held[:1]
            second_got = swapped(second)
        if q >= 0:
            held = apply_step(
                q, ints, floats, [environs[q + LAG * k] for k in range(SITES)], psi[0], right_env[0, 0], held)
    first_got = swapped(held[0])
    return reduced(held[0], first_got, second, second_got)


def solution(mesh):
    fine = Mesh(mesh.devices.reshape(4, 4, 4, 2), ("site", "z", "x", "core"))
    term = ("z", "x", "core")
    return jax.shard_map(
        shards,
        mesh=fine,
        in_specs=(
            P(term, None, None, None),
            P("site", term, None, None, None),
            P("site", None, None, None, None),
            P("site", None, None, None, None),
            P("site", term, None),
            P(),
            P(term, None),
        ),
        out_specs=P("site", None, term, None),
        check_vma=False,
    )
```
